32 devices in a mesh: gx: 4 (over y, x), gy: 8 (over z, core).
Axes of the slice: x: 2, y: 2, z: 4, core: 2. Of those that a mesh axis runs over, the one named last changes fastest.
Arguments:
- basis_fields: float32 [128, 128, 1024], P(None, 'gx', 'gy'), may hold values from -6 to 6
- carried_fields: float32 [128, 128, 1024], P(None, 'gx', 'gy'), may hold values from -70 to 70, as said below
- velocity: float32 [2, 128, 1024], P(None, 'gx', 'gy'), may hold values from -1 to 1
- diffusion: float32 [128, 128], replicated, may hold values from -0.024 to 0.09, as said below
- advection: float32 [128, 128], replicated, may hold values from -0.18 to 0.18
Outputs:
- new_basis: float32 [256, 128, 1024], P(None, 'gx', 'gy')
- galerkin: float32 [256, 128], replicated
The draws below stay inside these ranges and needn't reach their ends.
Inputs may be any that keep to these rules, and one draw needn't show every extreme that they name: `carried_fields`: entries of the field block are of order one with scales varying over cells and fields. `diffusion`: A positive diagonal with small couplings off it.
All inputs are finite; a program needn't handle non-finite values.
Results may differ from the reference program's by a relative error of at most 0.000086.
Values sent between devices are 32-bit elements; how exact they have to be, the bound alone decides.
No kernel may reach another device: no remote copies, remote signals or barrier semaphores. Data moves between devices by JAX's collectives and lax.ppermute only.
A program may use at most 64 MiB of HBM per device.

```python
import math
import jax
import jax.numpy as jnp
from jax import lax

R = 128
NX = 128
NY = 1024


def draw_carried_fields(key, part):
    key_base, key_rough, key_scale = jax.random.split(jax.random.fold_in(key, 11), 3)
    row_pos = jnp.arange(NX, dtype=jnp.float32) / NX
    col_pos = jnp.arange(NY, dtype=jnp.float32) / NY
    trend = (0.5 + 1.5 * row_pos)[:, None] * (0.7 + 0.6 * col_pos)[None, :]
    rough = jnp.exp(0.8 * jax.random.uniform(key_rough, (NX, NY), jnp.float32, -1.0, 1.0))
    field_scale = jnp.exp(jax.random.uniform(key_scale, (R,), jnp.float32, math.log(0.3), math.log(3.0)))
    base_draw = jax.random.truncated_normal(key_base, -4.0, 4.0, (R, NX, NY), jnp.float32)
    return base_draw * field_scale[:, None, None] * (trend * rough)[None, :, :]


def draw_diffusion(key, part):
    key_diag, key_off = jax.random.split(jax.random.fold_in(key, 23))
    diag_part = jax.random.uniform(key_diag, (R,), jnp.float32, 0.03, 0.09)
    off_part = 0.006 * jax.random.truncated_normal(key_off, -4.0, 4.0, (R, R), jnp.float32)
    identity = jnp.eye(R, dtype=jnp.float32)
    return off_part * (1.0 - identity) + identity * diag_part[None, :]


def shard_levels(own_key, dims, cuts, low, top_value):
    factor_of, own = 1.0, jax.random.fold_in(own_key, 6)
    for dim, parts in cuts:
        draws = jnp.exp(jax.random.uniform(jax.random.fold_in(own, dim), (parts,), jnp.float32, low / len(cuts), top_value / len(cuts)))
        factor_of = factor_of * jnp.repeat(draws, dims[dim] // parts).reshape([-1 if axis == dim else 1 for axis in range(len(dims))])
    return factor_of


def bell_draw(rng, dims, scale, bound, shards=(), kind=jnp.bfloat16):
    factor_of = shard_levels(rng, dims, shards, -0.22, 0.18) if shards else 1.0
    values = jax.random.normal(rng, dims, jnp.float32) * scale * factor_of
    return jnp.minimum(jnp.maximum(values, -bound), bound).astype(kind)


def setup_inputs(seed: int = 0) -> dict:
    key_of = jax.random.split(jax.random.key(seed), 6)
    basis_fields = bell_draw(key_of[0], (R, NX, NY), 1.0, 6.0, ((1, 4), (2, 8)), jnp.float32)
    carried_fields = draw_carried_fields(jax.random.fold_in(key_of[5], 71), 0)
    velocity = jnp.clip(jax.random.uniform(key_of[2], (2, NX, NY), jnp.float32, -1.0, 1.0) * shard_levels(key_of[2], (2, NX, NY), ((1, 4), (2, 8)), -0.4, 0.0), -1.0, 1.0)
    diffusion = draw_diffusion(jax.random.fold_in(key_of[5], 71), 0)
    advection = bell_draw(key_of[4], (R, R), 0.03, 0.18, (), jnp.float32)
    return dict(basis_fields=basis_fields, carried_fields=carried_fields, velocity=velocity, diffusion=diffusion, advection=advection)


def field_rate(fields, velocity, diffusion, advection):
    field_shape = fields.shape
    plus_x = jnp.roll(fields, -1, 1)
    minus_x = jnp.roll(fields, 1, 1)
    plus_y = jnp.roll(fields, -1, 2)
    minus_y = jnp.roll(fields, 1, 2)
    laplace = plus_x + minus_x + plus_y + minus_y - 4.0 * fields
    transport = velocity[0] * (plus_x - minus_x) * 0.5 + velocity[1] * (plus_y - minus_y) * 0.5
    spread_part = jnp.dot(diffusion.T, laplace.reshape(field_shape[0], -1), precision=lax.Precision.HIGHEST)
    carry_part = jnp.dot(advection.T, transport.reshape(field_shape[0], -1), precision=lax.Precision.HIGHEST)
    return (spread_part - carry_part).reshape(field_shape)

def reference(basis_fields, carried_fields, velocity, diffusion, advection):
    section_one = carried_fields + field_rate(carried_fields, velocity, diffusion, advection)
    section_two = section_one + field_rate(section_one, velocity, diffusion, advection)
    flat_new = section_two.reshape(R, -1)
    stacked = jnp.concatenate([basis_fields.reshape(R, -1), flat_new], 0)
    cell_weight = 1.0 / (NX * NY)
    gram_matrix = jnp.dot(stacked, stacked.T, precision=lax.Precision.HIGHEST) * cell_weight
    cholesky_low = jnp.linalg.cholesky(gram_matrix)
    new_basis = jax.scipy.linalg.solve_triangular(cholesky_low, stacked, lower=True)
    flat_carried = carried_fields.reshape(R, -1)
    galerkin = jnp.dot(new_basis, flat_carried.T, precision=lax.Precision.HIGHEST) * cell_weight
    return (new_basis.reshape(2 * R, NX, NY), galerkin)
```

```python
import jax
import jax.numpy as jnp
from jax import lax
from jax.sharding import PartitionSpec as P


def extended(array, sides, width):
    for axis, dim in sides:
        count, length = (lax.axis_size(axis), array.shape[dim])
        up = [(i, (i + 1) % count) for i in range(count)]
        down = [(j, i) for i, j in up]
        last = lax.slice_in_dim(array, length - width, length, axis=dim)
        first = lax.slice_in_dim(array, 0, width, axis=dim)
        before = lax.ppermute(last, axis, up)
        after = lax.ppermute(first, axis, down)
        array = jnp.concatenate([before, array, after], axis=dim)
    return array


def field_rate(padded, velocity, diffusion, advection):
    center = padded[:, 1:-1, 1:-1]
    plus_x = padded[:, 2:, 1:-1]
    minus_x = padded[:, :-2, 1:-1]
    plus_y = padded[:, 1:-1, 2:]
    minus_y = padded[:, 1:-1, :-2]
    field_shape = center.shape
    laplace = plus_x + minus_x + plus_y + minus_y - 4.0 * center
    transport = velocity[0] * (plus_x - minus_x) * 0.5 + velocity[1] * (plus_y - minus_y) * 0.5
    spread_part = jnp.dot(
        diffusion.T, laplace.reshape(field_shape[0], -1), precision=lax.Precision.HIGHEST
    )
    carry_part = jnp.dot(
        advection.T, transport.reshape(field_shape[0], -1), precision=lax.Precision.HIGHEST
    )
    return (spread_part - carry_part).reshape(field_shape)


def one_substep(fields, velocity, diffusion, advection):
    padded = extended(fields, (("gx", 1), ("gy", 2)), 1)
    return fields + field_rate(padded, velocity, diffusion, advection)


def body(basis_fields, carried_fields, velocity, diffusion, advection):
    basis_rank, tile_rows, tile_cols = carried_fields.shape
    tile_cells = tile_rows * tile_cols
    aug_count = 2 * basis_rank
    cell_weight = 1.0 / (tile_cells * lax.axis_size("gx") * lax.axis_size("gy"))
    flat_basis = basis_fields.reshape(basis_rank, tile_cells)
    flat_carried = carried_fields.reshape(basis_rank, tile_cells)
    section_one = one_substep(carried_fields, velocity, diffusion, advection)
    section_two = one_substep(section_one, velocity, diffusion, advection)
    flat_new = section_two.reshape(basis_rank, tile_cells)
    stacked = jnp.concatenate([flat_basis, flat_new], 0)
    both = jnp.concatenate([stacked, flat_carried], 0)
    whole_sum = lax.psum(jnp.dot(stacked, both.T, precision=lax.Precision.HIGHEST), ("gx", "gy"))
    gram_matrix = whole_sum[:, :aug_count] * cell_weight
    cholesky_low = jnp.linalg.cholesky(gram_matrix)
    identity = jnp.eye(aug_count, dtype=jnp.float32)
    inverse = jax.scipy.linalg.solve_triangular(cholesky_low, identity, lower=True)
    new_basis = jnp.dot(inverse, stacked, precision=lax.Precision.HIGHEST)
    galerkin = (
        jnp.dot(inverse, whole_sum[:, aug_count:], precision=lax.Precision.HIGHEST) * cell_weight
    )
    return (new_basis.reshape(aug_count, tile_rows, tile_cols), galerkin)


def solution(mesh):
    in_specs = (P(None, "gx", "gy"), P(None, "gx", "gy"), P(None, "gx", "gy"), P(), P())
    out_specs = (P(None, "gx", "gy"), P())
    return jax.shard_map(body, mesh=mesh, in_specs=in_specs, out_specs=out_specs, check_vma=False)
```

```python
import jax
import jax.numpy as jnp
from jax import lax
from jax.sharding import PartitionSpec as P


def extended(array, sides, width):
    for axis, dim in sides:
        count, length = (lax.axis_size(axis), array.shape[dim])
        up = [(i, (i + 1) % count) for i in range(count)]
        down = [(j, i) for i, j in up]
        last = lax.slice_in_dim(array, length - width, length, axis=dim)
        first = lax.slice_in_dim(array, 0, width, axis=dim)
        before = lax.ppermute(last, axis, up)
        after = lax.ppermute(first, axis, down)
        array = jnp.concatenate([before, array, after], axis=dim)
    return array


def exchange_sum(array, axes):
    for axis in axes:
        count, stride = lax.axis_size(axis), 1
        while stride < count:
            pairs = [(i, i ^ stride) for i in range(count)]
            array = array + lax.ppermute(array, axis, pairs)
            stride *= 2
    return array


def field_rate(padded, velocity, diffusion, advection):
    center = padded[:, 1:-1, 1:-1]
    plus_x = padded[:, 2:, 1:-1]
    minus_x = padded[:, :-2, 1:-1]
    plus_y = padded[:, 1:-1, 2:]
    minus_y = padded[:, 1:-1, :-2]
    field_shape = center.shape
    laplace = plus_x + minus_x + plus_y + minus_y - 4.0 * center
    transport = velocity[0] * (plus_x - minus_x) * 0.5 + velocity[1] * (plus_y - minus_y) * 0.5
    spread_part = jnp.dot(
        diffusion.T, laplace.reshape(field_shape[0], -1), precision=lax.Precision.HIGHEST
    )
    carry_part = jnp.dot(
        advection.T, transport.reshape(field_shape[0], -1), precision=lax.Precision.HIGHEST
    )
    return (spread_part - carry_part).reshape(field_shape)


def one_substep(fields, velocity, diffusion, advection):
    padded = extended(fields, (("gx", 1), ("gy", 2)), 1)
    return fields + field_rate(padded, velocity, diffusion, advection)


def body(basis_fields, carried_fields, velocity, diffusion, advection):
    basis_rank, tile_rows, tile_cols = carried_fields.shape
    tile_cells = tile_rows * tile_cols
    aug_count = 2 * basis_rank
    cell_weight = 1.0 / (tile_cells * lax.axis_size("gx") * lax.axis_size("gy"))
    flat_basis = basis_fields.reshape(basis_rank, tile_cells)
    flat_carried = carried_fields.reshape(basis_rank, tile_cells)
    section_one = one_substep(carried_fields, velocity, diffusion, advection)
    section_two = one_substep(section_one, velocity, diffusion, advection)
    flat_new = section_two.reshape(basis_rank, tile_cells)
    stacked = jnp.concatenate([flat_basis, flat_new], 0)
    both = jnp.concatenate([stacked, flat_carried], 0)
    whole_sum = exchange_sum(jnp.dot(stacked, both.T, precision=lax.Precision.HIGHEST), ("gy", "gx"))
    gram_matrix = whole_sum[:, :aug_count] * cell_weight
    cholesky_low = jnp.linalg.cholesky(gram_matrix)
    identity = jnp.eye(aug_count, dtype=jnp.float32)
    inverse = jax.scipy.linalg.solve_triangular(cholesky_low, identity, lower=True)
    new_basis = jnp.dot(inverse, stacked, precision=lax.Precision.HIGHEST)
    galerkin = (
        jnp.dot(inverse, whole_sum[:, aug_count:], precision=lax.Precision.HIGHEST) * cell_weight
    )
    return (new_basis.reshape(aug_count, tile_rows, tile_cols), galerkin)


def solution(mesh):
    in_specs = (P(None, "gx", "gy"), P(None, "gx", "gy"), P(None, "gx", "gy"), P(), P())
    out_specs = (P(None, "gx", "gy"), P())
    return jax.shard_map(body, mesh=mesh, in_specs=in_specs, out_specs=out_specs, check_vma=False)
```

```python
import jax
import jax.numpy as jnp
from jax import lax
from jax.sharding import PartitionSpec as P


def extended(array, sides, width):
    for axis, dim in sides:
        count, length = (lax.axis_size(axis), array.shape[dim])
        up = [(i, (i + 1) % count) for i in range(count)]
        down = [(j, i) for i, j in up]
        last = lax.slice_in_dim(array, length - width, length, axis=dim)
        first = lax.slice_in_dim(array, 0, width, axis=dim)
        before = lax.ppermute(last, axis, up)
        after = lax.ppermute(first, axis, down)
        array = jnp.concatenate([before, array, after], axis=dim)
    return array


def exchange_sum(array, axes):
    for axis in axes:
        count, stride = lax.axis_size(axis), 1
        while stride < count:
            pairs = [(i, i ^ stride) for i in range(count)]
            array = array + lax.ppermute(array, axis, pairs)
            stride *= 2
    return array


def field_rate(padded, velocity, diffusion, advection):
    center = padded[:, 1:-1, 1:-1]
    plus_x = padded[:, 2:, 1:-1]
    minus_x = padded[:, :-2, 1:-1]
    plus_y = padded[:, 1:-1, 2:]
    minus_y = padded[:, 1:-1, :-2]
    field_shape = center.shape
    laplace = plus_x + minus_x + plus_y + minus_y - 4.0 * center
    transport = velocity[0] * (plus_x - minus_x) * 0.5 + velocity[1] * (plus_y - minus_y) * 0.5
    spread_part = jnp.dot(
        diffusion.T, laplace.reshape(field_shape[0], -1), precision=lax.Precision.HIGHEST
    )
    carry_part = jnp.dot(
        advection.T, transport.reshape(field_shape[0], -1), precision=lax.Precision.HIGHEST
    )
    return (spread_part - carry_part).reshape(field_shape)


def one_substep(fields, velocity, diffusion, advection):
    padded = extended(fields, (("gx", 1), ("gy", 2)), 1)
    return fields + field_rate(padded, velocity, diffusion, advection)


def hdot(a, b):
    return jnp.dot(a, b, precision=lax.Precision.HIGHEST)


def lower_inverse(matrix):
    low = jnp.linalg.cholesky(matrix)
    identity = jnp.eye(matrix.shape[0], dtype=matrix.dtype)
    return jax.scipy.linalg.solve_triangular(low, identity, lower=True)


def body(basis_fields, carried_fields, velocity, diffusion, advection):
    basis_rank, tile_rows, tile_cols = carried_fields.shape
    tile_cells = tile_rows * tile_cols
    aug_count = 2 * basis_rank
    cell_weight = 1.0 / (tile_cells * lax.axis_size("gx") * lax.axis_size("gy"))
    axes = ("gy", "gx")
    flat_basis = basis_fields.reshape(basis_rank, tile_cells)
    flat_carried = carried_fields.reshape(basis_rank, tile_cells)
    known = jnp.concatenate([flat_basis, flat_carried], 0)
    basis_sum = exchange_sum(hdot(flat_basis, known.T), axes) * cell_weight
    section_one = one_substep(carried_fields, velocity, diffusion, advection)
    section_two = one_substep(section_one, velocity, diffusion, advection)
    flat_new = section_two.reshape(basis_rank, tile_cells)
    every = jnp.concatenate([flat_basis, flat_new, flat_carried], 0)
    new_sum = exchange_sum(hdot(flat_new, every.T), axes) * cell_weight
    inverse_11 = lower_inverse(basis_sum[:, :basis_rank])
    low_21 = hdot(new_sum[:, :basis_rank], inverse_11.T)
    schur = new_sum[:, basis_rank:aug_count] - hdot(low_21, low_21.T)
    inverse_22 = lower_inverse(schur)
    top = hdot(inverse_11, flat_basis)
    bottom = hdot(inverse_22, flat_new - hdot(low_21, top))
    new_basis = jnp.concatenate([top, bottom], 0)
    galerkin_top = hdot(inverse_11, basis_sum[:, basis_rank:])
    galerkin_bottom = hdot(inverse_22, new_sum[:, aug_count:] - hdot(low_21, galerkin_top))
    galerkin = jnp.concatenate([galerkin_top, galerkin_bottom], 0)
    return (new_basis.reshape(aug_count, tile_rows, tile_cols), galerkin)


def solution(mesh):
    in_specs = (P(None, "gx", "gy"), P(None, "gx", "gy"), P(None, "gx", "gy"), P(), P())
    out_specs = (P(None, "gx", "gy"), P())
    return jax.shard_map(body, mesh=mesh, in_specs=in_specs, out_specs=out_specs, check_vma=False)
```

```python
import jax
import jax.numpy as jnp
from jax import lax
from jax.sharding import PartitionSpec as P


def neighbour(array, axis, step):
    count = lax.axis_size(axis)
    pairs = [(i, (i + step) % count) for i in range(count)]
    return lax.ppermute(array, axis, pairs)


def exchange_sum(array, axes):
    for axis in axes:
        count, stride = lax.axis_size(axis), 1
        while stride < count:
            pairs = [(i, i ^ stride) for i in range(count)]
            array = array + lax.ppermute(array, axis, pairs)
            stride *= 2
    return array


def flat_substep(flat, speed_x, speed_y, coupling, rows, cols):
    count = flat.shape[0]
    grid = flat.reshape(count, rows, cols)
    above = neighbour(flat[:, (rows - 1) * cols:], "gx", 1)
    below = neighbour(flat[:, :cols], "gx", -1)
    left = neighbour(grid[:, :, cols - 1], "gy", 1)
    right = neighbour(grid[:, :, 0], "gy", -1)
    column = lax.broadcasted_iota(jnp.int32, (1, rows * cols), 1) % cols
    minus_x = jnp.concatenate([above, flat[:, : (rows - 1) * cols]], 1)
    plus_x = jnp.concatenate([flat[:, cols:], below], 1)
    plus_y = jnp.where(
        column == cols - 1,
        jnp.repeat(right, cols, axis=1),
        jnp.concatenate([flat[:, 1:], flat[:, :1]], 1),
    )
    minus_y = jnp.where(
        column == 0,
        jnp.repeat(left, cols, axis=1),
        jnp.concatenate([flat[:, -1:], flat[:, :-1]], 1),
    )
    laplace = plus_x + minus_x + plus_y + minus_y - 4.0 * flat
    transport = speed_x * (plus_x - minus_x) * 0.5 + speed_y * (plus_y - minus_y) * 0.5
    rate = hdot(coupling, jnp.concatenate([laplace, transport], 0))
    return flat + rate


def hdot(a, b):
    return jnp.dot(a, b, precision=lax.Precision.HIGHEST)


def lower_inverse(matrix):
    low = jnp.linalg.cholesky(matrix)
    identity = jnp.eye(matrix.shape[0], dtype=matrix.dtype)
    return jax.scipy.linalg.solve_triangular(low, identity, lower=True)


def body(basis_fields, carried_fields, velocity, diffusion, advection):
    basis_rank, tile_rows, tile_cols = carried_fields.shape
    tile_cells = tile_rows * tile_cols
    aug_count = 2 * basis_rank
    cell_weight = 1.0 / (tile_cells * lax.axis_size("gx") * lax.axis_size("gy"))
    axes = ("gy", "gx")
    flat_basis = basis_fields.reshape(basis_rank, tile_cells)
    flat_carried = carried_fields.reshape(basis_rank, tile_cells)
    known = jnp.concatenate([flat_basis, flat_carried], 0)
    basis_sum = exchange_sum(hdot(flat_basis, known.T), axes) * cell_weight
    flat_velocity = velocity.reshape(2, tile_cells)
    speed_x, speed_y = flat_velocity[0:1], flat_velocity[1:2]
    coupling = jnp.concatenate([diffusion.T, -advection.T], 1)
    section_one = flat_substep(flat_carried, speed_x, speed_y, coupling, tile_rows, tile_cols)
    flat_new = flat_substep(section_one, speed_x, speed_y, coupling, tile_rows, tile_cols)
    every = jnp.concatenate([flat_basis, flat_new, flat_carried], 0)
    new_sum = exchange_sum(hdot(flat_new, every.T), axes) * cell_weight
    inverse_11 = lower_inverse(basis_sum[:, :basis_rank])
    low_21 = hdot(new_sum[:, :basis_rank], inverse_11.T)
    schur = new_sum[:, basis_rank:aug_count] - hdot(low_21, low_21.T)
    inverse_22 = lower_inverse(schur)
    top = hdot(inverse_11, flat_basis)
    bottom = hdot(inverse_22, flat_new - hdot(low_21, top))
    new_basis = jnp.concatenate([top, bottom], 0)
    galerkin_top = hdot(inverse_11, basis_sum[:, basis_rank:])
    galerkin_bottom = hdot(inverse_22, new_sum[:, aug_count:] - hdot(low_21, galerkin_top))
    galerkin = jnp.concatenate([galerkin_top, galerkin_bottom], 0)
    return (new_basis.reshape(aug_count, tile_rows, tile_cols), galerkin)


def solution(mesh):
    in_specs = (P(None, "gx", "gy"), P(None, "gx", "gy"), P(None, "gx", "gy"), P(), P())
    out_specs = (P(None, "gx", "gy"), P())
    return jax.shard_map(body, mesh=mesh, in_specs=in_specs, out_specs=out_specs, check_vma=False)
```

```python
import functools
import jax
import jax.numpy as jnp
from jax import lax
from jax.experimental import pallas as pl
from jax.experimental.pallas import tpu as pltpu
from jax.sharding import PartitionSpec as P


def neighbour(array, axis, step):
    count = lax.axis_size(axis)
    pairs = [(i, (i + step) % count) for i in range(count)]
    return lax.ppermute(array, axis, pairs)


def substep_kernel(f_ref, above_ref, below_ref, left_ref, right_ref, vel_ref, mix_ref, out_ref,
                   *, count, rows, cols):
    col_id = lax.broadcasted_iota(jnp.int32, (count, cols), 1)
    coupling = mix_ref[...]

    def row_of(r):
        if r < 0:
            return above_ref[...]
        if r >= rows:
            return below_ref[...]
        return f_ref[pl.ds(r, count, stride=rows), :]

    prev, here = row_of(-1), row_of(0)
    for r in range(rows):
        nxt = row_of(r + 1)
        west = left_ref[:, r:r + 1]
        east = right_ref[:, r:r + 1]
        minus_y = jnp.where(col_id == 0, west, pltpu.roll(here, 1, 1))
        plus_y = jnp.where(col_id == cols - 1, east, pltpu.roll(here, cols - 1, 1))
        speed_x = vel_ref[r:r + 1, :]
        speed_y = vel_ref[rows + r:rows + r + 1, :]
        laplace = nxt + prev + plus_y + minus_y - 4.0 * here
        transport = speed_x * (nxt - prev) * 0.5 + speed_y * (plus_y - minus_y) * 0.5
        rate = jnp.dot(coupling, jnp.concatenate([laplace, transport], 0),
                       precision=lax.Precision.HIGHEST, preferred_element_type=jnp.float32)
        out_ref[pl.ds(r, count, stride=rows), :] = here + rate
        prev, here = here, nxt


def substep_call(flat, above, below, left, right, vel, coupling, count, rows, cols):
    vmem = pl.BlockSpec(memory_space=pltpu.VMEM)
    return pl.pallas_call(
        functools.partial(substep_kernel, count=count, rows=rows, cols=cols),
        out_shape=jax.ShapeDtypeStruct((count * rows, cols), jnp.float32),
        in_specs=[vmem] * 7,
        out_specs=vmem,
    )(flat, above, below, left, right, vel, coupling)


def one_substep(fields, flat_velocity, coupling):
    count, rows, cols = fields.shape
    above = neighbour(fields[:, rows - 1, :], "gx", 1)
    below = neighbour(fields[:, 0, :], "gx", -1)
    left = neighbour(fields[:, :, cols - 1], "gy", 1)
    right = neighbour(fields[:, :, 0], "gy", -1)
    flat = substep_call(
        fields.reshape(count * rows, cols), above, below, left, right, flat_velocity, coupling,
        count, rows, cols,
    )
    return flat.reshape(count, rows, cols)


def exchange_sum(array, axes):
    for axis in axes:
        count, stride = lax.axis_size(axis), 1
        while stride < count:
            pairs = [(i, i ^ stride) for i in range(count)]
            array = array + lax.ppermute(array, axis, pairs)
            stride *= 2
    return array


def hdot(a, b):
    return jnp.dot(a, b, precision=lax.Precision.HIGHEST)


def lower_inverse(matrix):
    low = jnp.linalg.cholesky(matrix)
    identity = jnp.eye(matrix.shape[0], dtype=matrix.dtype)
    return jax.scipy.linalg.solve_triangular(low, identity, lower=True)


def body(basis_fields, carried_fields, velocity, diffusion, advection):
    basis_rank, tile_rows, tile_cols = carried_fields.shape
    tile_cells = tile_rows * tile_cols
    aug_count = 2 * basis_rank
    cell_weight = 1.0 / (tile_cells * lax.axis_size("gx") * lax.axis_size("gy"))
    axes = ("gy", "gx")
    flat_basis = basis_fields.reshape(basis_rank, tile_cells)
    flat_carried = carried_fields.reshape(basis_rank, tile_cells)
    known = jnp.concatenate([flat_basis, flat_carried], 0)
    basis_sum = exchange_sum(hdot(flat_basis, known.T), axes) * cell_weight
    flat_velocity = velocity.reshape(2 * tile_rows, tile_cols)
    coupling = jnp.concatenate([diffusion.T, -advection.T], 1)
    section_one = one_substep(carried_fields, flat_velocity, coupling)
    section_two = one_substep(section_one, flat_velocity, coupling)
    flat_new = section_two.reshape(basis_rank, tile_cells)
    every = jnp.concatenate([flat_basis, flat_new, flat_carried], 0)
    new_sum = exchange_sum(hdot(flat_new, every.T), axes) * cell_weight
    inverse_11 = lower_inverse(basis_sum[:, :basis_rank])
    low_21 = hdot(new_sum[:, :basis_rank], inverse_11.T)
    schur = new_sum[:, basis_rank:aug_count] - hdot(low_21, low_21.T)
    inverse_22 = lower_inverse(schur)
    top = hdot(inverse_11, flat_basis)
    bottom = hdot(inverse_22, flat_new - hdot(low_21, top))
    new_basis = jnp.concatenate([top, bottom], 0)
    galerkin_top = hdot(inverse_11, basis_sum[:, basis_rank:])
    galerkin_bottom = hdot(inverse_22, new_sum[:, aug_count:] - hdot(low_21, galerkin_top))
    galerkin = jnp.concatenate([galerkin_top, galerkin_bottom], 0)
    return (new_basis.reshape(aug_count, tile_rows, tile_cols), galerkin)


def solution(mesh):
    in_specs = (P(None, "gx", "gy"), P(None, "gx", "gy"), P(None, "gx", "gy"), P(), P())
    out_specs = (P(None, "gx", "gy"), P())
    return jax.shard_map(body, mesh=mesh, in_specs=in_specs, out_specs=out_specs, check_vma=False)
```

```python
import functools
import jax
import jax.numpy as jnp
from jax import lax
from jax.experimental import pallas as pl
from jax.experimental.pallas import tpu as pltpu
from jax.sharding import PartitionSpec as P


def neighbour(array, axis, step):
    count = lax.axis_size(axis)
    pairs = [(i, (i + step) % count) for i in range(count)]
    return lax.ppermute(array, axis, pairs)


def keep_edges(r, block, top_ref, bottom_ref, first_ref, last_ref, rows, cols):
    if r == 0:
        top_ref[...] = block
    if r == rows - 1:
        bottom_ref[...] = block
    first_ref[:, r:r + 1] = block[:, 0:1]
    last_ref[:, r:r + 1] = block[:, cols - 1:cols]


def edges_kernel(f_ref, top_ref, bottom_ref, first_ref, last_ref, *, count, rows, cols):
    for r in range(rows):
        block = f_ref[pl.ds(r, count, stride=rows), :]
        keep_edges(r, block, top_ref, bottom_ref, first_ref, last_ref, rows, cols)


def substep_kernel(f_ref, above_ref, below_ref, left_ref, right_ref, vel_ref, mix_ref, out_ref,
                   top_ref, bottom_ref, first_ref, last_ref, *, count, rows, cols):
    col_id = lax.broadcasted_iota(jnp.int32, (count, cols), 1)
    coupling = mix_ref[...]

    def row_of(r):
        if r < 0:
            return above_ref[...]
        if r >= rows:
            return below_ref[...]
        return f_ref[pl.ds(r, count, stride=rows), :]

    prev, here = row_of(-1), row_of(0)
    for r in range(rows):
        nxt = row_of(r + 1)
        west = left_ref[:, r:r + 1]
        east = right_ref[:, r:r + 1]
        minus_y = jnp.where(col_id == 0, west, pltpu.roll(here, 1, 1))
        plus_y = jnp.where(col_id == cols - 1, east, pltpu.roll(here, cols - 1, 1))
        speed_x = vel_ref[r:r + 1, :]
        speed_y = vel_ref[rows + r:rows + r + 1, :]
        laplace = nxt + prev + plus_y + minus_y - 4.0 * here
        transport = speed_x * (nxt - prev) * 0.5 + speed_y * (plus_y - minus_y) * 0.5
        rate = jnp.dot(coupling, jnp.concatenate([laplace, transport], 0),
                       precision=lax.Precision.HIGHEST, preferred_element_type=jnp.float32)
        result = here + rate
        out_ref[pl.ds(r, count, stride=rows), :] = result
        keep_edges(r, result, top_ref, bottom_ref, first_ref, last_ref, rows, cols)
        prev, here = here, nxt


def edge_shapes(count, rows, cols):
    return [
        jax.ShapeDtypeStruct((count, cols), jnp.float32),
        jax.ShapeDtypeStruct((count, cols), jnp.float32),
        jax.ShapeDtypeStruct((count, rows), jnp.float32),
        jax.ShapeDtypeStruct((count, rows), jnp.float32),
    ]


def edges_call(flat, count, rows, cols):
    vmem = pl.BlockSpec(memory_space=pltpu.VMEM)
    return pl.pallas_call(
        functools.partial(edges_kernel, count=count, rows=rows, cols=cols),
        out_shape=edge_shapes(count, rows, cols),
        in_specs=[vmem],
        out_specs=[vmem] * 4,
    )(flat)


def substep_call(flat, above, below, left, right, vel, coupling, count, rows, cols):
    vmem = pl.BlockSpec(memory_space=pltpu.VMEM)
    return pl.pallas_call(
        functools.partial(substep_kernel, count=count, rows=rows, cols=cols),
        out_shape=[jax.ShapeDtypeStruct((count * rows, cols), jnp.float32)]
        + edge_shapes(count, rows, cols),
        in_specs=[vmem] * 7,
        out_specs=[vmem] * 5,
    )(flat, above, below, left, right, vel, coupling)


def one_substep(flat, edges, flat_velocity, coupling, count, rows, cols):
    top, bottom, first, last = edges
    above = neighbour(bottom, "gx", 1)
    below = neighbour(top, "gx", -1)
    left = neighbour(last, "gy", 1)
    right = neighbour(first, "gy", -1)
    result = substep_call(flat, above, below, left, right, flat_velocity, coupling, count, rows, cols)
    return result[0], result[1:]


def exchange_sum(array, axes):
    for axis in axes:
        count, stride = lax.axis_size(axis), 1
        while stride < count:
            pairs = [(i, i ^ stride) for i in range(count)]
            array = array + lax.ppermute(array, axis, pairs)
            stride *= 2
    return array


def hdot(a, b):
    return jnp.dot(a, b, precision=lax.Precision.HIGHEST)


def lower_inverse(matrix):
    low = jnp.linalg.cholesky(matrix)
    identity = jnp.eye(matrix.shape[0], dtype=matrix.dtype)
    return jax.scipy.linalg.solve_triangular(low, identity, lower=True)


def body(basis_fields, carried_fields, velocity, diffusion, advection):
    basis_rank, tile_rows, tile_cols = carried_fields.shape
    tile_cells = tile_rows * tile_cols
    aug_count = 2 * basis_rank
    cell_weight = 1.0 / (tile_cells * lax.axis_size("gx") * lax.axis_size("gy"))
    axes = ("gy", "gx")
    flat_basis = basis_fields.reshape(basis_rank, tile_cells)
    flat_carried = carried_fields.reshape(basis_rank, tile_cells)
    known = jnp.concatenate([flat_basis, flat_carried], 0)
    basis_sum = exchange_sum(hdot(flat_basis, known.T), axes) * cell_weight
    flat_velocity = velocity.reshape(2 * tile_rows, tile_cols)
    coupling = jnp.concatenate([diffusion.T, -advection.T], 1)
    shape = (basis_rank, tile_rows, tile_cols)
    carried_rows = carried_fields.reshape(basis_rank * tile_rows, tile_cols)
    edges = edges_call(carried_rows, *shape)
    section_one, edges = one_substep(carried_rows, edges, flat_velocity, coupling, *shape)
    section_two, _ = one_substep(section_one, edges, flat_velocity, coupling, *shape)
    flat_new = section_two.reshape(basis_rank, tile_cells)
    every = jnp.concatenate([flat_basis, flat_new, flat_carried], 0)
    new_sum = exchange_sum(hdot(flat_new, every.T), axes) * cell_weight
    inverse_11 = lower_inverse(basis_sum[:, :basis_rank])
    low_21 = hdot(new_sum[:, :basis_rank], inverse_11.T)
    schur = new_sum[:, basis_rank:aug_count] - hdot(low_21, low_21.T)
    inverse_22 = lower_inverse(schur)
    top = hdot(inverse_11, flat_basis)
    bottom = hdot(inverse_22, flat_new - hdot(low_21, top))
    new_basis = jnp.concatenate([top, bottom], 0)
    galerkin_top = hdot(inverse_11, basis_sum[:, basis_rank:])
    galerkin_bottom = hdot(inverse_22, new_sum[:, aug_count:] - hdot(low_21, galerkin_top))
    galerkin = jnp.concatenate([galerkin_top, galerkin_bottom], 0)
    return (new_basis.reshape(aug_count, tile_rows, tile_cols), galerkin)


def solution(mesh):
    in_specs = (P(None, "gx", "gy"), P(None, "gx", "gy"), P(None, "gx", "gy"), P(), P())
    out_specs = (P(None, "gx", "gy"), P())
    return jax.shard_map(body, mesh=mesh, in_specs=in_specs, out_specs=out_specs, check_vma=False)
```

```python
import functools
import jax
import jax.numpy as jnp
from jax import lax
from jax.experimental import pallas as pl
from jax.experimental.pallas import tpu as pltpu
from jax.sharding import PartitionSpec as P


def neighbour(array, axis, step):
    count = lax.axis_size(axis)
    pairs = [(i, (i + step) % count) for i in range(count)]
    return lax.ppermute(array, axis, pairs)


def keep_edges(r, block, top_ref, bottom_ref, first_ref, last_ref, rows, cols):
    if r == 0:
        top_ref[...] = block
    if r == rows - 1:
        bottom_ref[...] = block
    first_ref[:, r:r + 1] = block[:, 0:1]
    last_ref[:, r:r + 1] = block[:, cols - 1:cols]


def edges_kernel(f_ref, top_ref, bottom_ref, first_ref, last_ref, *, count, rows, cols):
    for r in range(rows):
        block = f_ref[pl.ds(r, count, stride=rows), :]
        keep_edges(r, block, top_ref, bottom_ref, first_ref, last_ref, rows, cols)


def substep_kernel(f_ref, above_ref, below_ref, left_ref, right_ref, vel_ref, mix_ref, out_ref,
                   top_ref, bottom_ref, first_ref, last_ref, *, count, rows, cols):
    col_id = lax.broadcasted_iota(jnp.int32, (count, cols), 1)
    coupling = mix_ref[...]

    def row_of(r):
        if r < 0:
            return above_ref[...]
        if r >= rows:
            return below_ref[...]
        return f_ref[pl.ds(r, count, stride=rows), :]

    prev, here = row_of(-1), row_of(0)
    for r in range(rows):
        nxt = row_of(r + 1)
        west = left_ref[:, r:r + 1]
        east = right_ref[:, r:r + 1]
        minus_y = jnp.where(col_id == 0, west, pltpu.roll(here, 1, 1))
        plus_y = jnp.where(col_id == cols - 1, east, pltpu.roll(here, cols - 1, 1))
        speed_x = vel_ref[r:r + 1, :]
        speed_y = vel_ref[rows + r:rows + r + 1, :]
        laplace = nxt + prev + plus_y + minus_y - 4.0 * here
        transport = speed_x * (nxt - prev) * 0.5 + speed_y * (plus_y - minus_y) * 0.5
        rate = jnp.dot(coupling, jnp.concatenate([laplace, transport], 0),
                       precision=lax.Precision.HIGHEST, preferred_element_type=jnp.float32)
        result = here + rate
        out_ref[pl.ds(r, count, stride=rows), :] = result
        keep_edges(r, result, top_ref, bottom_ref, first_ref, last_ref, rows, cols)
        prev, here = here, nxt


def edge_shapes(count, rows, cols):
    return [
        jax.ShapeDtypeStruct((count, cols), jnp.float32),
        jax.ShapeDtypeStruct((count, cols), jnp.float32),
        jax.ShapeDtypeStruct((count, rows), jnp.float32),
        jax.ShapeDtypeStruct((count, rows), jnp.float32),
    ]


def edges_call(flat, count, rows, cols):
    vmem = pl.BlockSpec(memory_space=pltpu.VMEM)
    return pl.pallas_call(
        functools.partial(edges_kernel, count=count, rows=rows, cols=cols),
        out_shape=edge_shapes(count, rows, cols),
        in_specs=[vmem],
        out_specs=[vmem] * 4,
    )(flat)


def substep_call(flat, above, below, left, right, vel, coupling, count, rows, cols):
    vmem = pl.BlockSpec(memory_space=pltpu.VMEM)
    return pl.pallas_call(
        functools.partial(substep_kernel, count=count, rows=rows, cols=cols),
        out_shape=[jax.ShapeDtypeStruct((count * rows, cols), jnp.float32)]
        + edge_shapes(count, rows, cols),
        in_specs=[vmem] * 7,
        out_specs=[vmem] * 5,
    )(flat, above, below, left, right, vel, coupling)


def one_substep(flat, edges, flat_velocity, coupling, count, rows, cols):
    top, bottom, first, last = edges
    above = neighbour(bottom, "gx", 1)
    below = neighbour(top, "gx", -1)
    left = neighbour(last, "gy", 1)
    right = neighbour(first, "gy", -1)
    result = substep_call(flat, above, below, left, right, flat_velocity, coupling, count, rows, cols)
    return result[0], result[1:]


def exchange_sum(array, axes):
    for axis in axes:
        count, stride = lax.axis_size(axis), 1
        while stride < count:
            pairs = [(i, i ^ stride) for i in range(count)]
            array = array + lax.ppermute(array, axis, pairs)
            stride *= 2
    return array


def hdot(a, b):
    return jnp.dot(a, b, precision=lax.Precision.HIGHEST)


def inverse_kernel(a_ref, x_ref, *, size):
    sub = lax.broadcasted_iota(jnp.int32, (size, size), 0)
    lane = lax.broadcasted_iota(jnp.int32, (size, size), 1)
    lane_row = lax.broadcasted_iota(jnp.int32, (1, size), 1)
    sub_col = lax.broadcasted_iota(jnp.int32, (size, 1), 0)

    def step(k, carry):
        a, x = carry
        row = jnp.sum(jnp.where(sub == k, a, 0.0), axis=0, keepdims=True)
        col = jnp.sum(jnp.where(lane == k, a, 0.0), axis=1, keepdims=True)
        pivot = jnp.sum(jnp.where(lane_row == k, row, 0.0), axis=1, keepdims=True)
        root = jnp.sqrt(pivot)
        low_row = jnp.where(lane_row >= k, row, 0.0) / root
        low_col = jnp.where(sub_col >= k, col, 0.0) / root
        x_row = jnp.sum(jnp.where(sub == k, x, 0.0), axis=0, keepdims=True) / root
        a = a - low_col * low_row
        x = jnp.where(sub == k, x_row, x - jnp.where(sub_col > k, low_col, 0.0) * x_row)
        return a, x

    eye = jnp.where(sub == lane, 1.0, 0.0).astype(jnp.float32)
    _, x = lax.fori_loop(0, size, step, (a_ref[...], eye), unroll=4)
    x_ref[...] = x


def lower_inverse_call(matrix):
    size = matrix.shape[0]
    vmem = pl.BlockSpec(memory_space=pltpu.VMEM)
    return pl.pallas_call(
        functools.partial(inverse_kernel, size=size),
        out_shape=jax.ShapeDtypeStruct((size, size), jnp.float32),
        in_specs=[vmem],
        out_specs=vmem,
    )(matrix)

def lower_inverse(matrix):
    return lower_inverse_call(0.5 * (matrix + matrix.T))


def body(basis_fields, carried_fields, velocity, diffusion, advection):
    basis_rank, tile_rows, tile_cols = carried_fields.shape
    tile_cells = tile_rows * tile_cols
    aug_count = 2 * basis_rank
    cell_weight = 1.0 / (tile_cells * lax.axis_size("gx") * lax.axis_size("gy"))
    axes = ("gy", "gx")
    flat_basis = basis_fields.reshape(basis_rank, tile_cells)
    flat_carried = carried_fields.reshape(basis_rank, tile_cells)
    known = jnp.concatenate([flat_basis, flat_carried], 0)
    basis_sum = exchange_sum(hdot(flat_basis, known.T), axes) * cell_weight
    flat_velocity = velocity.reshape(2 * tile_rows, tile_cols)
    coupling = jnp.concatenate([diffusion.T, -advection.T], 1)
    shape = (basis_rank, tile_rows, tile_cols)
    carried_rows = carried_fields.reshape(basis_rank * tile_rows, tile_cols)
    edges = edges_call(carried_rows, *shape)
    section_one, edges = one_substep(carried_rows, edges, flat_velocity, coupling, *shape)
    section_two, _ = one_substep(section_one, edges, flat_velocity, coupling, *shape)
    flat_new = section_two.reshape(basis_rank, tile_cells)
    every = jnp.concatenate([flat_basis, flat_new, flat_carried], 0)
    new_sum = exchange_sum(hdot(flat_new, every.T), axes) * cell_weight
    inverse_11 = lower_inverse(basis_sum[:, :basis_rank])
    low_21 = hdot(new_sum[:, :basis_rank], inverse_11.T)
    schur = new_sum[:, basis_rank:aug_count] - hdot(low_21, low_21.T)
    inverse_22 = lower_inverse(schur)
    top = hdot(inverse_11, flat_basis)
    bottom = hdot(inverse_22, flat_new - hdot(low_21, top))
    new_basis = jnp.concatenate([top, bottom], 0)
    galerkin_top = hdot(inverse_11, basis_sum[:, basis_rank:])
    galerkin_bottom = hdot(inverse_22, new_sum[:, aug_count:] - hdot(low_21, galerkin_top))
    galerkin = jnp.concatenate([galerkin_top, galerkin_bottom], 0)
    return (new_basis.reshape(aug_count, tile_rows, tile_cols), galerkin)


def solution(mesh):
    in_specs = (P(None, "gx", "gy"), P(None, "gx", "gy"), P(None, "gx", "gy"), P(), P())
    out_specs = (P(None, "gx", "gy"), P())
    return jax.shard_map(body, mesh=mesh, in_specs=in_specs, out_specs=out_specs, check_vma=False)
```

```python
import functools
import jax
import jax.numpy as jnp
from jax import lax
from jax.experimental import pallas as pl
from jax.experimental.pallas import tpu as pltpu
from jax.sharding import PartitionSpec as P


def neighbour(array, axis, step):
    count = lax.axis_size(axis)
    pairs = [(i, (i + step) % count) for i in range(count)]
    return lax.ppermute(array, axis, pairs)


def keep_edges(r, block, top_ref, bottom_ref, first_ref, last_ref, rows, cols):
    if r == 0:
        top_ref[...] = block
    if r == rows - 1:
        bottom_ref[...] = block
    first_ref[:, r:r + 1] = block[:, 0:1]
    last_ref[:, r:r + 1] = block[:, cols - 1:cols]


def edges_kernel(f_ref, top_ref, bottom_ref, first_ref, last_ref, *, count, rows, cols):
    for r in range(rows):
        block = f_ref[pl.ds(r, count, stride=rows), :]
        keep_edges(r, block, top_ref, bottom_ref, first_ref, last_ref, rows, cols)


def substep_kernel(f_ref, above_ref, below_ref, left_ref, right_ref, vel_ref, mix_ref, out_ref,
                   top_ref, bottom_ref, first_ref, last_ref, *, count, rows, cols):
    col_id = lax.broadcasted_iota(jnp.int32, (count, cols), 1)
    coupling = mix_ref[...]

    def row_of(r):
        if r < 0:
            return above_ref[...]
        if r >= rows:
            return below_ref[...]
        return f_ref[pl.ds(r, count, stride=rows), :]

    prev, here = row_of(-1), row_of(0)
    for r in range(rows):
        nxt = row_of(r + 1)
        west = left_ref[:, r:r + 1]
        east = right_ref[:, r:r + 1]
        minus_y = jnp.where(col_id == 0, west, pltpu.roll(here, 1, 1))
        plus_y = jnp.where(col_id == cols - 1, east, pltpu.roll(here, cols - 1, 1))
        speed_x = vel_ref[r:r + 1, :]
        speed_y = vel_ref[rows + r:rows + r + 1, :]
        laplace = nxt + prev + plus_y + minus_y - 4.0 * here
        transport = speed_x * (nxt - prev) * 0.5 + speed_y * (plus_y - minus_y) * 0.5
        rate = jnp.dot(coupling, jnp.concatenate([laplace, transport], 0),
                       precision=lax.Precision.HIGHEST, preferred_element_type=jnp.float32)
        result = here + rate
        out_ref[pl.ds(r, count, stride=rows), :] = result
        keep_edges(r, result, top_ref, bottom_ref, first_ref, last_ref, rows, cols)
        prev, here = here, nxt


def edge_shapes(count, rows, cols):
    return [
        jax.ShapeDtypeStruct((count, cols), jnp.float32),
        jax.ShapeDtypeStruct((count, cols), jnp.float32),
        jax.ShapeDtypeStruct((count, rows), jnp.float32),
        jax.ShapeDtypeStruct((count, rows), jnp.float32),
    ]


def edges_call(flat, count, rows, cols):
    vmem = pl.BlockSpec(memory_space=pltpu.VMEM)
    return pl.pallas_call(
        functools.partial(edges_kernel, count=count, rows=rows, cols=cols),
        out_shape=edge_shapes(count, rows, cols),
        in_specs=[vmem],
        out_specs=[vmem] * 4,
    )(flat)


def substep_call(flat, above, below, left, right, vel, coupling, count, rows, cols):
    vmem = pl.BlockSpec(memory_space=pltpu.VMEM)
    return pl.pallas_call(
        functools.partial(substep_kernel, count=count, rows=rows, cols=cols),
        out_shape=[jax.ShapeDtypeStruct((count * rows, cols), jnp.float32)]
        + edge_shapes(count, rows, cols),
        in_specs=[vmem] * 7,
        out_specs=[vmem] * 5,
    )(flat, above, below, left, right, vel, coupling)


def one_substep(flat, edges, flat_velocity, coupling, count, rows, cols):
    top, bottom, first, last = edges
    above = neighbour(bottom, "gx", 1)
    below = neighbour(top, "gx", -1)
    left = neighbour(last, "gy", 1)
    right = neighbour(first, "gy", -1)
    result = substep_call(flat, above, below, left, right, flat_velocity, coupling, count, rows, cols)
    return result[0], result[1:]


def exchange_sum(array, axes):
    for axis in axes:
        count, stride = lax.axis_size(axis), 1
        while stride < count:
            pairs = [(i, i ^ stride) for i in range(count)]
            array = array + lax.ppermute(array, axis, pairs)
            stride *= 2
    return array


def hdot(a, b):
    return jnp.dot(a, b, precision=lax.Precision.HIGHEST)


def inverse_kernel(a_ref, x_ref, *, size):
    sub = lax.broadcasted_iota(jnp.int32, (size, size), 0)
    lane = lax.broadcasted_iota(jnp.int32, (size, size), 1)
    lane_row = lax.broadcasted_iota(jnp.int32, (1, size), 1)
    sub_col = lax.broadcasted_iota(jnp.int32, (size, 1), 0)

    def step(k, carry):
        a, x = carry
        row = jnp.sum(jnp.where(sub == k, a, 0.0), axis=0, keepdims=True)
        col = jnp.sum(jnp.where(lane == k, a, 0.0), axis=1, keepdims=True)
        pivot = jnp.sum(jnp.where(lane_row == k, row, 0.0), axis=1, keepdims=True)
        scale = 1.0 / jnp.sqrt(pivot)
        low_row = jnp.where(lane_row >= k, row, 0.0) * scale
        low_col = jnp.where(sub_col >= k, col, 0.0) * scale
        x_row = jnp.sum(jnp.where(sub == k, x, 0.0), axis=0, keepdims=True) * scale
        a = a - low_col * low_row
        x = jnp.where(sub == k, x_row, x - jnp.where(sub_col > k, low_col, 0.0) * x_row)
        return a, x

    eye = jnp.where(sub == lane, 1.0, 0.0).astype(jnp.float32)
    _, x = lax.fori_loop(0, size, step, (a_ref[...], eye), unroll=4)
    x_ref[...] = x


def lower_inverse_call(matrix):
    size = matrix.shape[0]
    vmem = pl.BlockSpec(memory_space=pltpu.VMEM)
    return pl.pallas_call(
        functools.partial(inverse_kernel, size=size),
        out_shape=jax.ShapeDtypeStruct((size, size), jnp.float32),
        in_specs=[vmem],
        out_specs=vmem,
    )(matrix)

def lower_inverse(matrix):
    return lower_inverse_call(0.5 * (matrix + matrix.T))


def body(basis_fields, carried_fields, velocity, diffusion, advection):
    basis_rank, tile_rows, tile_cols = carried_fields.shape
    tile_cells = tile_rows * tile_cols
    aug_count = 2 * basis_rank
    cell_weight = 1.0 / (tile_cells * lax.axis_size("gx") * lax.axis_size("gy"))
    axes = ("gy", "gx")
    flat_basis = basis_fields.reshape(basis_rank, tile_cells)
    flat_carried = carried_fields.reshape(basis_rank, tile_cells)
    known = jnp.concatenate([flat_basis, flat_carried], 0)
    basis_sum = exchange_sum(hdot(flat_basis, known.T), axes) * cell_weight
    flat_velocity = velocity.reshape(2 * tile_rows, tile_cols)
    coupling = jnp.concatenate([diffusion.T, -advection.T], 1)
    shape = (basis_rank, tile_rows, tile_cols)
    carried_rows = carried_fields.reshape(basis_rank * tile_rows, tile_cols)
    edges = edges_call(carried_rows, *shape)
    section_one, edges = one_substep(carried_rows, edges, flat_velocity, coupling, *shape)
    section_two, _ = one_substep(section_one, edges, flat_velocity, coupling, *shape)
    flat_new = section_two.reshape(basis_rank, tile_cells)
    every = jnp.concatenate([flat_basis, flat_new, flat_carried], 0)
    new_sum = exchange_sum(hdot(flat_new, every.T), axes) * cell_weight
    inverse_11 = lower_inverse(basis_sum[:, :basis_rank])
    low_21 = hdot(new_sum[:, :basis_rank], inverse_11.T)
    schur = new_sum[:, basis_rank:aug_count] - hdot(low_21, low_21.T)
    inverse_22 = lower_inverse(schur)
    top = hdot(inverse_11, flat_basis)
    bottom = hdot(inverse_22, flat_new - hdot(low_21, top))
    new_basis = jnp.concatenate([top, bottom], 0)
    galerkin_top = hdot(inverse_11, basis_sum[:, basis_rank:])
    galerkin_bottom = hdot(inverse_22, new_sum[:, aug_count:] - hdot(low_21, galerkin_top))
    galerkin = jnp.concatenate([galerkin_top, galerkin_bottom], 0)
    return (new_basis.reshape(aug_count, tile_rows, tile_cols), galerkin)


def solution(mesh):
    in_specs = (P(None, "gx", "gy"), P(None, "gx", "gy"), P(None, "gx", "gy"), P(), P())
    out_specs = (P(None, "gx", "gy"), P())
    return jax.shard_map(body, mesh=mesh, in_specs=in_specs, out_specs=out_specs, check_vma=False)
```

```python
import functools
import jax
import jax.numpy as jnp
from jax import lax
from jax.experimental import pallas as pl
from jax.experimental.pallas import tpu as pltpu
from jax.sharding import PartitionSpec as P


def neighbour(array, axis, step):
    count = lax.axis_size(axis)
    pairs = [(i, (i + step) % count) for i in range(count)]
    return lax.ppermute(array, axis, pairs)


def keep_edges(r, block, top_ref, bottom_ref, first_ref, last_ref, rows, cols):
    if r == 0:
        top_ref[...] = block
    if r == rows - 1:
        bottom_ref[...] = block
    first_ref[:, r:r + 1] = block[:, 0:1]
    last_ref[:, r:r + 1] = block[:, cols - 1:cols]


def cell_products(left, right):
    return lax.dot_general(left, right, (((1,), (1,)), ((), ())),
                           precision=lax.Precision.HIGHEST, preferred_element_type=jnp.float32)


def edges_kernel(f_ref, b_ref, top_ref, bottom_ref, first_ref, last_ref, gram_ref, *, count, rows, cols):
    for r in range(rows):
        cells = pl.ds(r, count, stride=rows)
        block = f_ref[cells, :]
        keep_edges(r, block, top_ref, bottom_ref, first_ref, last_ref, rows, cols)
        basis = b_ref[cells, :]
        part = cell_products(basis, jnp.concatenate([basis, block], 0))
        if r == 0:
            gram_ref[...] = part
        else:
            gram_ref[...] += part


def substep_kernel(f_ref, above_ref, below_ref, left_ref, right_ref, vel_ref, mix_ref, *refs,
                   count, rows, cols, with_gram):
    if with_gram:
        b_ref, c_ref, out_ref, top_ref, bottom_ref, first_ref, last_ref, gram_ref = refs
    else:
        out_ref, top_ref, bottom_ref, first_ref, last_ref = refs
    col_id = lax.broadcasted_iota(jnp.int32, (count, cols), 1)
    coupling = mix_ref[...]

    def row_of(r):
        if r < 0:
            return above_ref[...]
        if r >= rows:
            return below_ref[...]
        return f_ref[pl.ds(r, count, stride=rows), :]

    prev, here = row_of(-1), row_of(0)
    for r in range(rows):
        nxt = row_of(r + 1)
        west = left_ref[:, r:r + 1]
        east = right_ref[:, r:r + 1]
        minus_y = jnp.where(col_id == 0, west, pltpu.roll(here, 1, 1))
        plus_y = jnp.where(col_id == cols - 1, east, pltpu.roll(here, cols - 1, 1))
        speed_x = vel_ref[r:r + 1, :]
        speed_y = vel_ref[rows + r:rows + r + 1, :]
        laplace = nxt + prev + plus_y + minus_y - 4.0 * here
        transport = speed_x * (nxt - prev) * 0.5 + speed_y * (plus_y - minus_y) * 0.5
        rate = jnp.dot(coupling, jnp.concatenate([laplace, transport], 0),
                       precision=lax.Precision.HIGHEST, preferred_element_type=jnp.float32)
        result = here + rate
        out_ref[pl.ds(r, count, stride=rows), :] = result
        keep_edges(r, result, top_ref, bottom_ref, first_ref, last_ref, rows, cols)
        if with_gram:
            cells = pl.ds(r, count, stride=rows)
            every = jnp.concatenate([b_ref[cells, :], result, c_ref[cells, :]], 0)
            part = cell_products(result, every)
            if r == 0:
                gram_ref[...] = part
            else:
                gram_ref[...] += part
        prev, here = here, nxt


def edge_shapes(count, rows, cols):
    return [
        jax.ShapeDtypeStruct((count, cols), jnp.float32),
        jax.ShapeDtypeStruct((count, cols), jnp.float32),
        jax.ShapeDtypeStruct((count, rows), jnp.float32),
        jax.ShapeDtypeStruct((count, rows), jnp.float32),
    ]


def edges_call(flat, basis, count, rows, cols):
    vmem = pl.BlockSpec(memory_space=pltpu.VMEM)
    return pl.pallas_call(
        functools.partial(edges_kernel, count=count, rows=rows, cols=cols),
        out_shape=edge_shapes(count, rows, cols)
        + [jax.ShapeDtypeStruct((count, 2 * count), jnp.float32)],
        in_specs=[vmem] * 2,
        out_specs=[vmem] * 5,
    )(flat, basis)


def substep_call(flat, above, below, left, right, vel, coupling, count, rows, cols, extra=()):
    vmem = pl.BlockSpec(memory_space=pltpu.VMEM)
    with_gram = bool(extra)
    gram = [jax.ShapeDtypeStruct((count, 3 * count), jnp.float32)] if with_gram else []
    return pl.pallas_call(
        functools.partial(substep_kernel, count=count, rows=rows, cols=cols, with_gram=with_gram),
        out_shape=[jax.ShapeDtypeStruct((count * rows, cols), jnp.float32)]
        + edge_shapes(count, rows, cols) + gram,
        in_specs=[vmem] * (7 + len(extra)),
        out_specs=[vmem] * (5 + len(gram)),
    )(flat, above, below, left, right, vel, coupling, *extra)


def one_substep(flat, edges, flat_velocity, coupling, count, rows, cols, extra=()):
    top, bottom, first, last = edges
    above = neighbour(bottom, "gx", 1)
    below = neighbour(top, "gx", -1)
    left = neighbour(last, "gy", 1)
    right = neighbour(first, "gy", -1)
    result = substep_call(flat, above, below, left, right, flat_velocity, coupling, count, rows, cols,
                          extra)
    return result[0], result[1:5], result[5:]


def exchange_sum(array, axes):
    for axis in axes:
        count, stride = lax.axis_size(axis), 1
        while stride < count:
            pairs = [(i, i ^ stride) for i in range(count)]
            array = array + lax.ppermute(array, axis, pairs)
            stride *= 2
    return array


def hdot(a, b):
    return jnp.dot(a, b, precision=lax.Precision.HIGHEST)


def inverse_kernel(a_ref, x_ref, *, size):
    sub = lax.broadcasted_iota(jnp.int32, (size, size), 0)
    lane = lax.broadcasted_iota(jnp.int32, (size, size), 1)
    lane_row = lax.broadcasted_iota(jnp.int32, (1, size), 1)
    sub_col = lax.broadcasted_iota(jnp.int32, (size, 1), 0)

    def step(k, carry):
        a, x = carry
        row = jnp.sum(jnp.where(sub == k, a, 0.0), axis=0, keepdims=True)
        col = jnp.sum(jnp.where(lane == k, a, 0.0), axis=1, keepdims=True)
        pivot = jnp.sum(jnp.where(lane_row == k, row, 0.0), axis=1, keepdims=True)
        root = jnp.sqrt(pivot)
        low_row = jnp.where(lane_row >= k, row, 0.0) / root
        low_col = jnp.where(sub_col >= k, col, 0.0) / root
        x_row = jnp.sum(jnp.where(sub == k, x, 0.0), axis=0, keepdims=True) / root
        a = a - low_col * low_row
        x = jnp.where(sub == k, x_row, x - jnp.where(sub_col > k, low_col, 0.0) * x_row)
        return a, x

    eye = jnp.where(sub == lane, 1.0, 0.0).astype(jnp.float32)
    _, x = lax.fori_loop(0, size, step, (a_ref[...], eye), unroll=4)
    x_ref[...] = x


def lower_inverse_call(matrix):
    size = matrix.shape[0]
    vmem = pl.BlockSpec(memory_space=pltpu.VMEM)
    return pl.pallas_call(
        functools.partial(inverse_kernel, size=size),
        out_shape=jax.ShapeDtypeStruct((size, size), jnp.float32),
        in_specs=[vmem],
        out_specs=vmem,
    )(matrix)

def lower_inverse(matrix):
    return lower_inverse_call(0.5 * (matrix + matrix.T))


def body(basis_fields, carried_fields, velocity, diffusion, advection):
    basis_rank, tile_rows, tile_cols = carried_fields.shape
    tile_cells = tile_rows * tile_cols
    aug_count = 2 * basis_rank
    cell_weight = 1.0 / (tile_cells * lax.axis_size("gx") * lax.axis_size("gy"))
    axes = ("gy", "gx")
    flat_basis = basis_fields.reshape(basis_rank, tile_cells)
    flat_carried = carried_fields.reshape(basis_rank, tile_cells)
    flat_velocity = velocity.reshape(2 * tile_rows, tile_cols)
    coupling = jnp.concatenate([diffusion.T, -advection.T], 1)
    shape = (basis_rank, tile_rows, tile_cols)
    carried_rows = carried_fields.reshape(basis_rank * tile_rows, tile_cols)
    basis_rows = basis_fields.reshape(basis_rank * tile_rows, tile_cols)
    *edges, basis_part = edges_call(carried_rows, basis_rows, *shape)
    basis_sum = exchange_sum(basis_part, axes) * cell_weight
    section_one, edges, _ = one_substep(carried_rows, edges, flat_velocity, coupling, *shape)
    section_two, _, (new_part,) = one_substep(
        section_one, edges, flat_velocity, coupling, *shape, extra=(basis_rows, carried_rows)
    )
    flat_new = section_two.reshape(basis_rank, tile_cells)
    new_sum = exchange_sum(new_part, axes) * cell_weight
    inverse_11 = lower_inverse(basis_sum[:, :basis_rank])
    low_21 = hdot(new_sum[:, :basis_rank], inverse_11.T)
    schur = new_sum[:, basis_rank:aug_count] - hdot(low_21, low_21.T)
    inverse_22 = lower_inverse(schur)
    top = hdot(inverse_11, flat_basis)
    bottom = hdot(inverse_22, flat_new - hdot(low_21, top))
    new_basis = jnp.concatenate([top, bottom], 0)
    galerkin_top = hdot(inverse_11, basis_sum[:, basis_rank:])
    galerkin_bottom = hdot(inverse_22, new_sum[:, aug_count:] - hdot(low_21, galerkin_top))
    galerkin = jnp.concatenate([galerkin_top, galerkin_bottom], 0)
    return (new_basis.reshape(aug_count, tile_rows, tile_cols), galerkin)


def solution(mesh):
    in_specs = (P(None, "gx", "gy"), P(None, "gx", "gy"), P(None, "gx", "gy"), P(), P())
    out_specs = (P(None, "gx", "gy"), P())
    return jax.shard_map(body, mesh=mesh, in_specs=in_specs, out_specs=out_specs, check_vma=False)
```

```python
import functools
import jax
import jax.numpy as jnp
from jax import lax
from jax.experimental import pallas as pl
from jax.experimental.pallas import tpu as pltpu
from jax.sharding import PartitionSpec as P


def neighbour(array, axis, step):
    count = lax.axis_size(axis)
    pairs = [(i, (i + step) % count) for i in range(count)]
    return lax.ppermute(array, axis, pairs)


def keep_edges(r, block, top_ref, bottom_ref, first_ref, last_ref, rows, cols):
    if r == 0:
        top_ref[...] = block
    if r == rows - 1:
        bottom_ref[...] = block
    first_ref[:, r:r + 1] = block[:, 0:1]
    last_ref[:, r:r + 1] = block[:, cols - 1:cols]


def cell_products(left, right):
    return lax.dot_general(left, right, (((1,), (1,)), ((), ())),
                           precision=lax.Precision.HIGHEST, preferred_element_type=jnp.float32)


def edges_kernel(f_ref, b_ref, top_ref, bottom_ref, first_ref, last_ref, gram_ref, *, count, rows, cols):
    for r in range(rows):
        cells = pl.ds(r, count, stride=rows)
        block = f_ref[cells, :]
        keep_edges(r, block, top_ref, bottom_ref, first_ref, last_ref, rows, cols)
        basis = b_ref[cells, :]
        part = cell_products(basis, jnp.concatenate([basis, block], 0))
        if r == 0:
            gram_ref[...] = part
        else:
            gram_ref[...] += part


def substep_kernel(f_ref, above_ref, below_ref, left_ref, right_ref, vel_ref, mix_ref, *refs,
                   count, rows, cols, with_gram):
    if with_gram:
        b_ref, c_ref, out_ref, top_ref, bottom_ref, first_ref, last_ref, gram_ref = refs
    else:
        out_ref, top_ref, bottom_ref, first_ref, last_ref = refs
    col_id = lax.broadcasted_iota(jnp.int32, (count, cols), 1)
    coupling = mix_ref[...]

    def row_of(r):
        if r < 0:
            return above_ref[...]
        if r >= rows:
            return below_ref[...]
        return f_ref[pl.ds(r, count, stride=rows), :]

    prev, here = row_of(-1), row_of(0)
    for r in range(rows):
        nxt = row_of(r + 1)
        west = left_ref[:, r:r + 1]
        east = right_ref[:, r:r + 1]
        minus_y = jnp.where(col_id == 0, west, pltpu.roll(here, 1, 1))
        plus_y = jnp.where(col_id == cols - 1, east, pltpu.roll(here, cols - 1, 1))
        speed_x = vel_ref[r:r + 1, :]
        speed_y = vel_ref[rows + r:rows + r + 1, :]
        laplace = nxt + prev + plus_y + minus_y - 4.0 * here
        transport = speed_x * (nxt - prev) * 0.5 + speed_y * (plus_y - minus_y) * 0.5
        rate = jnp.dot(coupling, jnp.concatenate([laplace, transport], 0),
                       precision=lax.Precision.HIGHEST, preferred_element_type=jnp.float32)
        result = here + rate
        out_ref[pl.ds(r, count, stride=rows), :] = result
        keep_edges(r, result, top_ref, bottom_ref, first_ref, last_ref, rows, cols)
        if with_gram:
            cells = pl.ds(r, count, stride=rows)
            every = jnp.concatenate([b_ref[cells, :], result, c_ref[cells, :]], 0)
            part = cell_products(result, every)
            if r == 0:
                gram_ref[...] = part
            else:
                gram_ref[...] += part
        prev, here = here, nxt


def edge_shapes(count, rows, cols):
    return [
        jax.ShapeDtypeStruct((count, cols), jnp.float32),
        jax.ShapeDtypeStruct((count, cols), jnp.float32),
        jax.ShapeDtypeStruct((count, rows), jnp.float32),
        jax.ShapeDtypeStruct((count, rows), jnp.float32),
    ]


def edges_call(flat, basis, count, rows, cols):
    vmem = pl.BlockSpec(memory_space=pltpu.VMEM)
    return pl.pallas_call(
        functools.partial(edges_kernel, count=count, rows=rows, cols=cols),
        out_shape=edge_shapes(count, rows, cols)
        + [jax.ShapeDtypeStruct((count, 2 * count), jnp.float32)],
        in_specs=[vmem] * 2,
        out_specs=[vmem] * 5,
    )(flat, basis)


def substep_call(flat, above, below, left, right, vel, coupling, count, rows, cols, extra=()):
    vmem = pl.BlockSpec(memory_space=pltpu.VMEM)
    with_gram = bool(extra)
    gram = [jax.ShapeDtypeStruct((count, 3 * count), jnp.float32)] if with_gram else []
    return pl.pallas_call(
        functools.partial(substep_kernel, count=count, rows=rows, cols=cols, with_gram=with_gram),
        out_shape=[jax.ShapeDtypeStruct((count * rows, cols), jnp.float32)]
        + edge_shapes(count, rows, cols) + gram,
        in_specs=[vmem] * (7 + len(extra)),
        out_specs=[vmem] * (5 + len(gram)),
    )(flat, above, below, left, right, vel, coupling, *extra)


def one_substep(flat, edges, flat_velocity, coupling, count, rows, cols, extra=()):
    top, bottom, first, last = edges
    above = neighbour(bottom, "gx", 1)
    below = neighbour(top, "gx", -1)
    left = neighbour(last, "gy", 1)
    right = neighbour(first, "gy", -1)
    result = substep_call(flat, above, below, left, right, flat_velocity, coupling, count, rows, cols,
                          extra)
    return result[0], result[1:5], result[5:]


def exchange_sum(array, axes):
    for axis in axes:
        count, stride = lax.axis_size(axis), 1
        while stride < count:
            pairs = [(i, i ^ stride) for i in range(count)]
            array = array + lax.ppermute(array, axis, pairs)
            stride *= 2
    return array


def hdot(a, b):
    return jnp.dot(a, b, precision=lax.Precision.HIGHEST)


def inverse_kernel(a_ref, x_ref, *, size):
    sub = lax.broadcasted_iota(jnp.int32, (size, size), 0)
    lane = lax.broadcasted_iota(jnp.int32, (size, size), 1)
    lane_row = lax.broadcasted_iota(jnp.int32, (1, size), 1)
    sub_col = lax.broadcasted_iota(jnp.int32, (size, 1), 0)

    def step(k, carry):
        a, x = carry
        row = jnp.sum(jnp.where(sub == k, a, 0.0), axis=0, keepdims=True)
        col = jnp.sum(jnp.where(lane == k, a, 0.0), axis=1, keepdims=True)
        pivot = jnp.sum(jnp.where(lane_row == k, row, 0.0), axis=1, keepdims=True)
        root = jnp.sqrt(pivot)
        low_row = jnp.where(lane_row >= k, row, 0.0) / root
        low_col = jnp.where(sub_col >= k, col, 0.0) / root
        x_row = jnp.sum(jnp.where(sub == k, x, 0.0), axis=0, keepdims=True) / root
        a = a - low_col * low_row
        x = jnp.where(sub == k, x_row, x - jnp.where(sub_col > k, low_col, 0.0) * x_row)
        return a, x

    eye = jnp.where(sub == lane, 1.0, 0.0).astype(jnp.float32)
    _, x = lax.fori_loop(0, size, step, (a_ref[...], eye), unroll=4)
    x_ref[...] = x


def lower_inverse_call(matrix):
    size = matrix.shape[0]
    vmem = pl.BlockSpec(memory_space=pltpu.VMEM)
    return pl.pallas_call(
        functools.partial(inverse_kernel, size=size),
        out_shape=jax.ShapeDtypeStruct((size, size), jnp.float32),
        in_specs=[vmem],
        out_specs=vmem,
    )(matrix)

def lower_inverse(matrix):
    return lower_inverse_call(0.5 * (matrix + matrix.T))


def body(basis_fields, carried_fields, velocity, diffusion, advection):
    basis_rank, tile_rows, tile_cols = carried_fields.shape
    tile_cells = tile_rows * tile_cols
    aug_count = 2 * basis_rank
    cell_weight = 1.0 / (tile_cells * lax.axis_size("gx") * lax.axis_size("gy"))
    axes = ("gy", "gx")
    flat_basis = basis_fields.reshape(basis_rank, tile_cells)
    flat_carried = carried_fields.reshape(basis_rank, tile_cells)
    flat_velocity = velocity.reshape(2 * tile_rows, tile_cols)
    coupling = jnp.concatenate([diffusion.T, -advection.T], 1)
    shape = (basis_rank, tile_rows, tile_cols)
    carried_rows = carried_fields.reshape(basis_rank * tile_rows, tile_cols)
    basis_rows = basis_fields.reshape(basis_rank * tile_rows, tile_cols)
    *edges, basis_part = edges_call(carried_rows, basis_rows, *shape)
    basis_sum = exchange_sum(basis_part, axes) * cell_weight
    section_one, edges, _ = one_substep(carried_rows, edges, flat_velocity, coupling, *shape)
    section_two, _, _ = one_substep(section_one, edges, flat_velocity, coupling, *shape)
    flat_new = section_two.reshape(basis_rank, tile_cells)
    every = jnp.concatenate([flat_basis, flat_new, flat_carried], 0)
    new_sum = exchange_sum(hdot(flat_new, every.T), axes) * cell_weight
    inverse_11 = lower_inverse(basis_sum[:, :basis_rank])
    low_21 = hdot(new_sum[:, :basis_rank], inverse_11.T)
    schur = new_sum[:, basis_rank:aug_count] - hdot(low_21, low_21.T)
    inverse_22 = lower_inverse(schur)
    top = hdot(inverse_11, flat_basis)
    bottom = hdot(inverse_22, flat_new - hdot(low_21, top))
    new_basis = jnp.concatenate([top, bottom], 0)
    galerkin_top = hdot(inverse_11, basis_sum[:, basis_rank:])
    galerkin_bottom = hdot(inverse_22, new_sum[:, aug_count:] - hdot(low_21, galerkin_top))
    galerkin = jnp.concatenate([galerkin_top, galerkin_bottom], 0)
    return (new_basis.reshape(aug_count, tile_rows, tile_cols), galerkin)


def solution(mesh):
    in_specs = (P(None, "gx", "gy"), P(None, "gx", "gy"), P(None, "gx", "gy"), P(), P())
    out_specs = (P(None, "gx", "gy"), P())
    return jax.shard_map(body, mesh=mesh, in_specs=in_specs, out_specs=out_specs, check_vma=False)
```

```python
import functools
import jax
import jax.numpy as jnp
from jax import lax
from jax.experimental import pallas as pl
from jax.experimental.pallas import tpu as pltpu
from jax.sharding import PartitionSpec as P


def neighbour(array, axis, step):
    count = lax.axis_size(axis)
    pairs = [(i, (i + step) % count) for i in range(count)]
    return lax.ppermute(array, axis, pairs)


def keep_edges(r, block, top_ref, bottom_ref, first_ref, last_ref, rows, cols):
    if r == 0:
        top_ref[...] = block
    if r == rows - 1:
        bottom_ref[...] = block
    first_ref[:, r:r + 1] = block[:, 0:1]
    last_ref[:, r:r + 1] = block[:, cols - 1:cols]


def edges_kernel(f_ref, top_ref, bottom_ref, first_ref, last_ref, *, count, rows, cols):
    for r in range(rows):
        block = f_ref[pl.ds(r, count, stride=rows), :]
        keep_edges(r, block, top_ref, bottom_ref, first_ref, last_ref, rows, cols)


def substep_kernel(f_ref, above_ref, below_ref, left_ref, right_ref, vel_ref, mix_ref, out_ref,
                   top_ref, bottom_ref, first_ref, last_ref, *, count, rows, cols):
    col_id = lax.broadcasted_iota(jnp.int32, (count, cols), 1)
    coupling = mix_ref[...]

    def row_of(r):
        if r < 0:
            return above_ref[...]
        if r >= rows:
            return below_ref[...]
        return f_ref[pl.ds(r, count, stride=rows), :]

    prev, here = row_of(-1), row_of(0)
    for r in range(rows):
        nxt = row_of(r + 1)
        west = left_ref[:, r:r + 1]
        east = right_ref[:, r:r + 1]
        minus_y = jnp.where(col_id == 0, west, pltpu.roll(here, 1, 1))
        plus_y = jnp.where(col_id == cols - 1, east, pltpu.roll(here, cols - 1, 1))
        speed_x = vel_ref[r:r + 1, :]
        speed_y = vel_ref[rows + r:rows + r + 1, :]
        laplace = nxt + prev + plus_y + minus_y - 4.0 * here
        transport = speed_x * (nxt - prev) * 0.5 + speed_y * (plus_y - minus_y) * 0.5
        rate = jnp.dot(coupling, jnp.concatenate([laplace, transport], 0),
                       precision=lax.Precision.HIGHEST, preferred_element_type=jnp.float32)
        result = here + rate
        out_ref[pl.ds(r, count, stride=rows), :] = result
        keep_edges(r, result, top_ref, bottom_ref, first_ref, last_ref, rows, cols)
        prev, here = here, nxt


def edge_shapes(count, rows, cols):
    return [
        jax.ShapeDtypeStruct((count, cols), jnp.float32),
        jax.ShapeDtypeStruct((count, cols), jnp.float32),
        jax.ShapeDtypeStruct((count, rows), jnp.float32),
        jax.ShapeDtypeStruct((count, rows), jnp.float32),
    ]


def edges_call(flat, count, rows, cols):
    vmem = pl.BlockSpec(memory_space=pltpu.VMEM)
    return pl.pallas_call(
        functools.partial(edges_kernel, count=count, rows=rows, cols=cols),
        out_shape=edge_shapes(count, rows, cols),
        in_specs=[vmem],
        out_specs=[vmem] * 4,
    )(flat)


def substep_call(flat, above, below, left, right, vel, coupling, count, rows, cols):
    vmem = pl.BlockSpec(memory_space=pltpu.VMEM)
    return pl.pallas_call(
        functools.partial(substep_kernel, count=count, rows=rows, cols=cols),
        out_shape=[jax.ShapeDtypeStruct((count * rows, cols), jnp.float32)]
        + edge_shapes(count, rows, cols),
        in_specs=[vmem] * 7,
        out_specs=[vmem] * 5,
    )(flat, above, below, left, right, vel, coupling)


def one_substep(flat, edges, flat_velocity, coupling, count, rows, cols):
    top, bottom, first, last = edges
    above = neighbour(bottom, "gx", 1)
    below = neighbour(top, "gx", -1)
    left = neighbour(last, "gy", 1)
    right = neighbour(first, "gy", -1)
    result = substep_call(flat, above, below, left, right, flat_velocity, coupling, count, rows, cols)
    return result[0], result[1:]


def exchange_sum(array, axes):
    for axis in axes:
        count, stride = lax.axis_size(axis), 1
        while stride < count:
            pairs = [(i, i ^ stride) for i in range(count)]
            array = array + lax.ppermute(array, axis, pairs)
            stride *= 2
    return array


def hdot(a, b):
    return jnp.dot(a, b, precision=lax.Precision.HIGHEST)


def inverse_kernel(a_ref, x_ref, *, size):
    sub = lax.broadcasted_iota(jnp.int32, (size, size), 0)
    lane = lax.broadcasted_iota(jnp.int32, (size, size), 1)
    lane_row = lax.broadcasted_iota(jnp.int32, (1, size), 1)
    sub_col = lax.broadcasted_iota(jnp.int32, (size, 1), 0)

    def row_at(m, k):
        return jnp.sum(jnp.where(sub == k, m, 0.0), axis=0, keepdims=True)

    def col_at(m, k):
        return jnp.sum(jnp.where(lane == k, m, 0.0), axis=1, keepdims=True)

    def lane_at(v, k):
        return jnp.sum(jnp.where(lane_row == k, v, 0.0), axis=1, keepdims=True)

    def step(k, carry):
        a, x, row, col, x_raw = carry
        scale = 1.0 / jnp.sqrt(lane_at(row, k))
        cross = lane_at(row, k + 1) * scale
        low_row = jnp.where(lane_row >= k, row, 0.0) * scale
        low_col = jnp.where(sub_col >= k, col, 0.0) * scale
        x_row = x_raw * scale
        next_row = row_at(a, k + 1) - cross * low_row
        next_col = col_at(a, k + 1) - cross * low_col
        next_x = row_at(x, k + 1) - cross * x_row
        a = a - low_col * low_row
        x = jnp.where(sub == k, x_row, x - jnp.where(sub_col > k, low_col, 0.0) * x_row)
        return a, x, next_row, next_col, next_x

    a0 = a_ref[...]
    eye = jnp.where(sub == lane, 1.0, 0.0).astype(jnp.float32)
    init = (a0, eye, row_at(a0, 0), col_at(a0, 0), row_at(eye, 0))
    x = lax.fori_loop(0, size, step, init, unroll=4)[1]
    x_ref[...] = x


def lower_inverse_call(matrix):
    size = matrix.shape[0]
    vmem = pl.BlockSpec(memory_space=pltpu.VMEM)
    return pl.pallas_call(
        functools.partial(inverse_kernel, size=size),
        out_shape=jax.ShapeDtypeStruct((size, size), jnp.float32),
        in_specs=[vmem],
        out_specs=vmem,
    )(matrix)

def lower_inverse(matrix):
    return lower_inverse_call(0.5 * (matrix + matrix.T))


def body(basis_fields, carried_fields, velocity, diffusion, advection):
    basis_rank, tile_rows, tile_cols = carried_fields.shape
    tile_cells = tile_rows * tile_cols
    aug_count = 2 * basis_rank
    cell_weight = 1.0 / (tile_cells * lax.axis_size("gx") * lax.axis_size("gy"))
    axes = ("gy", "gx")
    flat_basis = basis_fields.reshape(basis_rank, tile_cells)
    flat_carried = carried_fields.reshape(basis_rank, tile_cells)
    known = jnp.concatenate([flat_basis, flat_carried], 0)
    basis_sum = exchange_sum(hdot(flat_basis, known.T), axes) * cell_weight
    flat_velocity = velocity.reshape(2 * tile_rows, tile_cols)
    coupling = jnp.concatenate([diffusion.T, -advection.T], 1)
    shape = (basis_rank, tile_rows, tile_cols)
    carried_rows = carried_fields.reshape(basis_rank * tile_rows, tile_cols)
    edges = edges_call(carried_rows, *shape)
    section_one, edges = one_substep(carried_rows, edges, flat_velocity, coupling, *shape)
    section_two, _ = one_substep(section_one, edges, flat_velocity, coupling, *shape)
    flat_new = section_two.reshape(basis_rank, tile_cells)
    every = jnp.concatenate([flat_basis, flat_new, flat_carried], 0)
    new_sum = exchange_sum(hdot(flat_new, every.T), axes) * cell_weight
    inverse_11 = lower_inverse(basis_sum[:, :basis_rank])
    low_21 = hdot(new_sum[:, :basis_rank], inverse_11.T)
    schur = new_sum[:, basis_rank:aug_count] - hdot(low_21, low_21.T)
    inverse_22 = lower_inverse(schur)
    top = hdot(inverse_11, flat_basis)
    bottom = hdot(inverse_22, flat_new - hdot(low_21, top))
    new_basis = jnp.concatenate([top, bottom], 0)
    galerkin_top = hdot(inverse_11, basis_sum[:, basis_rank:])
    galerkin_bottom = hdot(inverse_22, new_sum[:, aug_count:] - hdot(low_21, galerkin_top))
    galerkin = jnp.concatenate([galerkin_top, galerkin_bottom], 0)
    return (new_basis.reshape(aug_count, tile_rows, tile_cols), galerkin)


def solution(mesh):
    in_specs = (P(None, "gx", "gy"), P(None, "gx", "gy"), P(None, "gx", "gy"), P(), P())
    out_specs = (P(None, "gx", "gy"), P())
    return jax.shard_map(body, mesh=mesh, in_specs=in_specs, out_specs=out_specs, check_vma=False)
```

```python
import functools
import jax
import jax.numpy as jnp
from jax import lax
from jax.experimental import pallas as pl
from jax.experimental.pallas import tpu as pltpu
from jax.sharding import PartitionSpec as P


def neighbour(array, axis, step):
    count = lax.axis_size(axis)
    pairs = [(i, (i + step) % count) for i in range(count)]
    return lax.ppermute(array, axis, pairs)


def keep_edges(r, block, top_ref, bottom_ref, first_ref, last_ref, rows, cols):
    if r == 0:
        top_ref[...] = block
    if r == rows - 1:
        bottom_ref[...] = block
    first_ref[:, r:r + 1] = block[:, 0:1]
    last_ref[:, r:r + 1] = block[:, cols - 1:cols]


def edges_kernel(f_ref, top_ref, bottom_ref, first_ref, last_ref, *, count, rows, cols):
    for r in range(rows):
        block = f_ref[pl.ds(r, count, stride=rows), :]
        keep_edges(r, block, top_ref, bottom_ref, first_ref, last_ref, rows, cols)


def substep_kernel(f_ref, above_ref, below_ref, left_ref, right_ref, vel_ref, mix_ref, out_ref,
                   top_ref, bottom_ref, first_ref, last_ref, *, count, rows, cols):
    col_id = lax.broadcasted_iota(jnp.int32, (count, cols), 1)
    coupling = mix_ref[...]

    def row_of(r):
        if r < 0:
            return above_ref[...]
        if r >= rows:
            return below_ref[...]
        return f_ref[pl.ds(r, count, stride=rows), :]

    prev, here = row_of(-1), row_of(0)
    for r in range(rows):
        nxt = row_of(r + 1)
        west = left_ref[:, r:r + 1]
        east = right_ref[:, r:r + 1]
        minus_y = jnp.where(col_id == 0, west, pltpu.roll(here, 1, 1))
        plus_y = jnp.where(col_id == cols - 1, east, pltpu.roll(here, cols - 1, 1))
        speed_x = vel_ref[r:r + 1, :]
        speed_y = vel_ref[rows + r:rows + r + 1, :]
        laplace = nxt + prev + plus_y + minus_y - 4.0 * here
        transport = speed_x * (nxt - prev) * 0.5 + speed_y * (plus_y - minus_y) * 0.5
        rate = jnp.dot(coupling, jnp.concatenate([laplace, transport], 0),
                       precision=lax.Precision.HIGHEST, preferred_element_type=jnp.float32)
        result = here + rate
        out_ref[pl.ds(r, count, stride=rows), :] = result
        keep_edges(r, result, top_ref, bottom_ref, first_ref, last_ref, rows, cols)
        prev, here = here, nxt


def edge_shapes(count, rows, cols):
    return [
        jax.ShapeDtypeStruct((count, cols), jnp.float32),
        jax.ShapeDtypeStruct((count, cols), jnp.float32),
        jax.ShapeDtypeStruct((count, rows), jnp.float32),
        jax.ShapeDtypeStruct((count, rows), jnp.float32),
    ]


def edges_call(flat, count, rows, cols):
    vmem = pl.BlockSpec(memory_space=pltpu.VMEM)
    return pl.pallas_call(
        functools.partial(edges_kernel, count=count, rows=rows, cols=cols),
        out_shape=edge_shapes(count, rows, cols),
        in_specs=[vmem],
        out_specs=[vmem] * 4,
    )(flat)


def substep_call(flat, above, below, left, right, vel, coupling, count, rows, cols):
    vmem = pl.BlockSpec(memory_space=pltpu.VMEM)
    return pl.pallas_call(
        functools.partial(substep_kernel, count=count, rows=rows, cols=cols),
        out_shape=[jax.ShapeDtypeStruct((count * rows, cols), jnp.float32)]
        + edge_shapes(count, rows, cols),
        in_specs=[vmem] * 7,
        out_specs=[vmem] * 5,
    )(flat, above, below, left, right, vel, coupling)


def one_substep(flat, edges, flat_velocity, coupling, count, rows, cols):
    top, bottom, first, last = edges
    above = neighbour(bottom, "gx", 1)
    below = neighbour(top, "gx", -1)
    left = neighbour(last, "gy", 1)
    right = neighbour(first, "gy", -1)
    result = substep_call(flat, above, below, left, right, flat_velocity, coupling, count, rows, cols)
    return result[0], result[1:]


def exchange_sum(array, axes, last=None):
    stages = []
    for axis in axes:
        count, stride = lax.axis_size(axis), 1
        while stride < count:
            stages.append((axis, stride))
            stride *= 2
    if last in stages:
        stages.remove(last)
        stages.append(last)
    for axis, stride in stages:
        pairs = [(i, i ^ stride) for i in range(lax.axis_size(axis))]
        array = array + lax.ppermute(array, axis, pairs)
    return array


def hdot(a, b):
    return jnp.dot(a, b, precision=lax.Precision.HIGHEST)


def inverse_kernel(a_ref, x_ref, *, size):
    sub = lax.broadcasted_iota(jnp.int32, (size, size), 0)
    lane = lax.broadcasted_iota(jnp.int32, (size, size), 1)
    lane_row = lax.broadcasted_iota(jnp.int32, (1, size), 1)
    sub_col = lax.broadcasted_iota(jnp.int32, (size, 1), 0)

    def row_at(m, k):
        return jnp.sum(jnp.where(sub == k, m, 0.0), axis=0, keepdims=True)

    def col_at(m, k):
        return jnp.sum(jnp.where(lane == k, m, 0.0), axis=1, keepdims=True)

    def lane_at(v, k):
        return jnp.sum(jnp.where(lane_row == k, v, 0.0), axis=1, keepdims=True)

    def step(k, carry):
        a, x, row, col, x_raw = carry
        scale = 1.0 / jnp.sqrt(lane_at(row, k))
        cross = lane_at(row, k + 1) * scale
        low_row = jnp.where(lane_row >= k, row, 0.0) * scale
        low_col = jnp.where(sub_col >= k, col, 0.0) * scale
        x_row = x_raw * scale
        next_row = row_at(a, k + 1) - cross * low_row
        next_col = col_at(a, k + 1) - cross * low_col
        next_x = row_at(x, k + 1) - cross * x_row
        a = a - low_col * low_row
        x = jnp.where(sub == k, x_row, x - jnp.where(sub_col > k, low_col, 0.0) * x_row)
        return a, x, next_row, next_col, next_x

    a0 = a_ref[...]
    eye = jnp.where(sub == lane, 1.0, 0.0).astype(jnp.float32)
    init = (a0, eye, row_at(a0, 0), col_at(a0, 0), row_at(eye, 0))
    x = lax.fori_loop(0, size, step, init, unroll=4)[1]
    x_ref[...] = x


def lower_inverse_call(matrix):
    size = matrix.shape[0]
    vmem = pl.BlockSpec(memory_space=pltpu.VMEM)
    return pl.pallas_call(
        functools.partial(inverse_kernel, size=size),
        out_shape=jax.ShapeDtypeStruct((size, size), jnp.float32),
        in_specs=[vmem],
        out_specs=vmem,
    )(matrix)

def lower_inverse(matrix):
    return lower_inverse_call(0.5 * (matrix + matrix.T))


def body(basis_fields, carried_fields, velocity, diffusion, advection):
    basis_rank, tile_rows, tile_cols = carried_fields.shape
    tile_cells = tile_rows * tile_cols
    aug_count = 2 * basis_rank
    cell_weight = 1.0 / (tile_cells * lax.axis_size("gx") * lax.axis_size("gy"))
    axes = ("gy", "gx")
    flat_basis = basis_fields.reshape(basis_rank, tile_cells)
    flat_carried = carried_fields.reshape(basis_rank, tile_cells)
    known = jnp.concatenate([flat_basis, flat_carried], 0)
    basis_sum = exchange_sum(hdot(flat_basis, known.T), axes) * cell_weight
    flat_velocity = velocity.reshape(2 * tile_rows, tile_cols)
    coupling = jnp.concatenate([diffusion.T, -advection.T], 1)
    shape = (basis_rank, tile_rows, tile_cols)
    carried_rows = carried_fields.reshape(basis_rank * tile_rows, tile_cols)
    edges = edges_call(carried_rows, *shape)
    section_one, edges = one_substep(carried_rows, edges, flat_velocity, coupling, *shape)
    section_two, _ = one_substep(section_one, edges, flat_velocity, coupling, *shape)
    flat_new = section_two.reshape(basis_rank, tile_cells)
    every = jnp.concatenate([flat_basis, flat_new, flat_carried], 0)
    new_sum = exchange_sum(hdot(flat_new, every.T), axes, last=("gy", 1)) * cell_weight
    inverse_11 = lower_inverse(basis_sum[:, :basis_rank])
    low_21 = hdot(new_sum[:, :basis_rank], inverse_11.T)
    schur = new_sum[:, basis_rank:aug_count] - hdot(low_21, low_21.T)
    inverse_22 = lower_inverse(schur)
    top = hdot(inverse_11, flat_basis)
    bottom = hdot(inverse_22, flat_new - hdot(low_21, top))
    new_basis = jnp.concatenate([top, bottom], 0)
    galerkin_top = hdot(inverse_11, basis_sum[:, basis_rank:])
    galerkin_bottom = hdot(inverse_22, new_sum[:, aug_count:] - hdot(low_21, galerkin_top))
    galerkin = jnp.concatenate([galerkin_top, galerkin_bottom], 0)
    return (new_basis.reshape(aug_count, tile_rows, tile_cols), galerkin)


def solution(mesh):
    in_specs = (P(None, "gx", "gy"), P(None, "gx", "gy"), P(None, "gx", "gy"), P(), P())
    out_specs = (P(None, "gx", "gy"), P())
    return jax.shard_map(body, mesh=mesh, in_specs=in_specs, out_specs=out_specs, check_vma=False)
```

```python
import functools
import jax
import jax.numpy as jnp
from jax import lax
from jax.experimental import pallas as pl
from jax.experimental.pallas import tpu as pltpu
from jax.sharding import PartitionSpec as P


def neighbour(array, axis, step):
    count = lax.axis_size(axis)
    pairs = [(i, (i + step) % count) for i in range(count)]
    return lax.ppermute(array, axis, pairs)


def keep_edges(r, block, top_ref, bottom_ref, first_ref, last_ref, rows, cols):
    if r == 0:
        top_ref[...] = block
    if r == rows - 1:
        bottom_ref[...] = block
    first_ref[:, r:r + 1] = block[:, 0:1]
    last_ref[:, r:r + 1] = block[:, cols - 1:cols]


def edges_kernel(f_ref, top_ref, bottom_ref, first_ref, last_ref, *, count, rows, cols):
    for r in range(rows):
        block = f_ref[pl.ds(r, count, stride=rows), :]
        keep_edges(r, block, top_ref, bottom_ref, first_ref, last_ref, rows, cols)


def substep_kernel(f_ref, above_ref, below_ref, left_ref, right_ref, vel_ref, mix_ref, out_ref,
                   top_ref, bottom_ref, first_ref, last_ref, *, count, rows, cols):
    col_id = lax.broadcasted_iota(jnp.int32, (count, cols), 1)
    coupling = mix_ref[...]

    def row_of(r):
        if r < 0:
            return above_ref[...]
        if r >= rows:
            return below_ref[...]
        return f_ref[pl.ds(r, count, stride=rows), :]

    prev, here = row_of(-1), row_of(0)
    for r in range(rows):
        nxt = row_of(r + 1)
        west = left_ref[:, r:r + 1]
        east = right_ref[:, r:r + 1]
        minus_y = jnp.where(col_id == 0, west, pltpu.roll(here, 1, 1))
        plus_y = jnp.where(col_id == cols - 1, east, pltpu.roll(here, cols - 1, 1))
        speed_x = vel_ref[r:r + 1, :]
        speed_y = vel_ref[rows + r:rows + r + 1, :]
        laplace = nxt + prev + plus_y + minus_y - 4.0 * here
        transport = speed_x * (nxt - prev) * 0.5 + speed_y * (plus_y - minus_y) * 0.5
        rate = jnp.dot(coupling, jnp.concatenate([laplace, transport], 0),
                       precision=lax.Precision.HIGHEST, preferred_element_type=jnp.float32)
        result = here + rate
        out_ref[pl.ds(r, count, stride=rows), :] = result
        keep_edges(r, result, top_ref, bottom_ref, first_ref, last_ref, rows, cols)
        prev, here = here, nxt


def edge_shapes(count, rows, cols):
    return [
        jax.ShapeDtypeStruct((count, cols), jnp.float32),
        jax.ShapeDtypeStruct((count, cols), jnp.float32),
        jax.ShapeDtypeStruct((count, rows), jnp.float32),
        jax.ShapeDtypeStruct((count, rows), jnp.float32),
    ]


def edges_call(flat, count, rows, cols):
    vmem = pl.BlockSpec(memory_space=pltpu.VMEM)
    return pl.pallas_call(
        functools.partial(edges_kernel, count=count, rows=rows, cols=cols),
        out_shape=edge_shapes(count, rows, cols),
        in_specs=[vmem],
        out_specs=[vmem] * 4,
    )(flat)


def substep_call(flat, above, below, left, right, vel, coupling, count, rows, cols):
    vmem = pl.BlockSpec(memory_space=pltpu.VMEM)
    return pl.pallas_call(
        functools.partial(substep_kernel, count=count, rows=rows, cols=cols),
        out_shape=[jax.ShapeDtypeStruct((count * rows, cols), jnp.float32)]
        + edge_shapes(count, rows, cols),
        in_specs=[vmem] * 7,
        out_specs=[vmem] * 5,
    )(flat, above, below, left, right, vel, coupling)


def one_substep(flat, edges, flat_velocity, coupling, count, rows, cols):
    top, bottom, first, last = edges
    above = neighbour(bottom, "gx", 1)
    below = neighbour(top, "gx", -1)
    left = neighbour(last, "gy", 1)
    right = neighbour(first, "gy", -1)
    result = substep_call(flat, above, below, left, right, flat_velocity, coupling, count, rows, cols)
    return result[0], result[1:]


def exchange_sum(array, axes, last=None):
    stages = []
    for axis in axes:
        count, stride = lax.axis_size(axis), 1
        while stride < count:
            stages.append((axis, stride))
            stride *= 2
    if last in stages:
        stages.remove(last)
        stages.append(last)
    for axis, stride in stages:
        pairs = [(i, i ^ stride) for i in range(lax.axis_size(axis))]
        array = array + lax.ppermute(array, axis, pairs)
    return array


def hdot(a, b):
    return jnp.dot(a, b, precision=lax.Precision.HIGHEST)


def inverse_kernel(a_ref, x_ref, *, size):
    sub = lax.broadcasted_iota(jnp.int32, (size, size), 0)
    lane = lax.broadcasted_iota(jnp.int32, (size, size), 1)
    lane_row = lax.broadcasted_iota(jnp.int32, (1, size), 1)
    sub_col = lax.broadcasted_iota(jnp.int32, (size, 1), 0)

    def row_at(m, k):
        return jnp.sum(jnp.where(sub == k, m, 0.0), axis=0, keepdims=True)

    def col_at(m, k):
        return jnp.sum(jnp.where(lane == k, m, 0.0), axis=1, keepdims=True)

    def lane_at(v, k):
        return jnp.sum(jnp.where(lane_row == k, v, 0.0), axis=1, keepdims=True)

    def step(k, carry):
        a, x, row, col, x_raw = carry
        scale = 1.0 / jnp.sqrt(lane_at(row, k))
        cross = lane_at(row, k + 1) * scale
        low_row = jnp.where(lane_row >= k, row, 0.0) * scale
        low_col = jnp.where(sub_col >= k, col, 0.0) * scale
        x_row = x_raw * scale
        next_row = row_at(a, k + 1) - cross * low_row
        next_col = col_at(a, k + 1) - cross * low_col
        next_x = row_at(x, k + 1) - cross * x_row
        a = a - low_col * low_row
        x = jnp.where(sub == k, x_row, x - jnp.where(sub_col > k, low_col, 0.0) * x_row)
        return a, x, next_row, next_col, next_x

    a0 = a_ref[...]
    eye = jnp.where(sub == lane, 1.0, 0.0).astype(jnp.float32)
    init = (a0, eye, row_at(a0, 0), col_at(a0, 0), row_at(eye, 0))
    x = lax.fori_loop(0, size, step, init, unroll=4)[1]
    x_ref[...] = x


def lower_inverse_call(matrix):
    size = matrix.shape[0]
    vmem = pl.BlockSpec(memory_space=pltpu.VMEM)
    return pl.pallas_call(
        functools.partial(inverse_kernel, size=size),
        out_shape=jax.ShapeDtypeStruct((size, size), jnp.float32),
        in_specs=[vmem],
        out_specs=vmem,
    )(matrix)

def lower_inverse(matrix):
    return lower_inverse_call(0.5 * (matrix + matrix.T))


def body(basis_fields, carried_fields, velocity, diffusion, advection):
    basis_rank, tile_rows, tile_cols = carried_fields.shape
    tile_cells = tile_rows * tile_cols
    aug_count = 2 * basis_rank
    cell_weight = 1.0 / (tile_cells * lax.axis_size("gx") * lax.axis_size("gy"))
    axes = ("gy", "gx")
    flat_basis = basis_fields.reshape(basis_rank, tile_cells)
    flat_carried = carried_fields.reshape(basis_rank, tile_cells)
    known = jnp.concatenate([flat_basis, flat_carried], 0)
    basis_sum = exchange_sum(hdot(flat_basis, known.T), axes) * cell_weight
    flat_velocity = velocity.reshape(2 * tile_rows, tile_cols)
    coupling = jnp.concatenate([diffusion.T, -advection.T], 1)
    shape = (basis_rank, tile_rows, tile_cols)
    carried_rows = carried_fields.reshape(basis_rank * tile_rows, tile_cols)
    edges = edges_call(carried_rows, *shape)
    section_one, edges = one_substep(carried_rows, edges, flat_velocity, coupling, *shape)
    section_two, _ = one_substep(section_one, edges, flat_velocity, coupling, *shape)
    flat_new = section_two.reshape(basis_rank, tile_cells)
    every = jnp.concatenate([flat_basis, flat_new, flat_carried], 0)
    new_sum = exchange_sum(hdot(flat_new, every.T), axes, last=("gy", 1)) * cell_weight
    inverse_11 = lower_inverse(basis_sum[:, :basis_rank])
    low_21 = hdot(new_sum[:, :basis_rank], inverse_11.T)
    schur = new_sum[:, basis_rank:aug_count] - hdot(low_21, low_21.T)
    inverse_22 = lower_inverse(schur)
    cross = hdot(inverse_22, hdot(low_21, inverse_11))
    zeros = jnp.zeros_like(inverse_11)
    inverse = jnp.concatenate(
        [jnp.concatenate([inverse_11, zeros], 1), jnp.concatenate([-cross, inverse_22], 1)], 0
    )
    new_basis = hdot(inverse, jnp.concatenate([flat_basis, flat_new], 0))
    galerkin = hdot(inverse, jnp.concatenate([basis_sum[:, basis_rank:], new_sum[:, aug_count:]], 0))
    return (new_basis.reshape(aug_count, tile_rows, tile_cols), galerkin)


def solution(mesh):
    in_specs = (P(None, "gx", "gy"), P(None, "gx", "gy"), P(None, "gx", "gy"), P(), P())
    out_specs = (P(None, "gx", "gy"), P())
    return jax.shard_map(body, mesh=mesh, in_specs=in_specs, out_specs=out_specs, check_vma=False)
```

```python
import functools
import jax
import jax.numpy as jnp
from jax import lax
from jax.experimental import pallas as pl
from jax.experimental.pallas import tpu as pltpu
from jax.sharding import PartitionSpec as P


def neighbour(array, axis, step):
    count = lax.axis_size(axis)
    pairs = [(i, (i + step) % count) for i in range(count)]
    return lax.ppermute(array, axis, pairs)


def keep_edges(r, block, top_ref, bottom_ref, first_ref, last_ref, rows, cols):
    if r == 0:
        top_ref[...] = block
    if r == rows - 1:
        bottom_ref[...] = block
    first_ref[:, r:r + 1] = block[:, 0:1]
    last_ref[:, r:r + 1] = block[:, cols - 1:cols]


def edges_kernel(f_ref, top_ref, bottom_ref, first_ref, last_ref, *, count, rows, cols):
    for r in range(rows):
        block = f_ref[pl.ds(r, count, stride=rows), :]
        keep_edges(r, block, top_ref, bottom_ref, first_ref, last_ref, rows, cols)


def substep_kernel(f_ref, above_ref, below_ref, left_ref, right_ref, vel_ref, mix_ref, out_ref,
                   top_ref, bottom_ref, first_ref, last_ref, *, count, rows, cols):
    col_id = lax.broadcasted_iota(jnp.int32, (count, cols), 1)
    coupling = mix_ref[...]

    def row_of(r):
        if r < 0:
            return above_ref[...]
        if r >= rows:
            return below_ref[...]
        return f_ref[pl.ds(r, count, stride=rows), :]

    def stencil(r, prev, here, nxt):
        west = left_ref[:, r:r + 1]
        east = right_ref[:, r:r + 1]
        minus_y = jnp.where(col_id == 0, west, pltpu.roll(here, 1, 1))
        plus_y = jnp.where(col_id == cols - 1, east, pltpu.roll(here, cols - 1, 1))
        speed_x = vel_ref[r:r + 1, :]
        speed_y = vel_ref[rows + r:rows + r + 1, :]
        laplace = nxt + prev + plus_y + minus_y - 4.0 * here
        transport = speed_x * (nxt - prev) * 0.5 + speed_y * (plus_y - minus_y) * 0.5
        return jnp.concatenate([laplace, transport], 0)

    blocks = [row_of(r) for r in range(-1, rows + 1)]
    group = 2 if rows % 2 == 0 else 1
    for r in range(0, rows, group):
        stacks = [stencil(r + g, blocks[r + g], blocks[r + g + 1], blocks[r + g + 2])
                  for g in range(group)]
        rate = jnp.dot(coupling, jnp.concatenate(stacks, 1),
                       precision=lax.Precision.HIGHEST, preferred_element_type=jnp.float32)
        for g in range(group):
            result = blocks[r + g + 1] + rate[:, g * cols:(g + 1) * cols]
            out_ref[pl.ds(r + g, count, stride=rows), :] = result
            keep_edges(r + g, result, top_ref, bottom_ref, first_ref, last_ref, rows, cols)


def edge_shapes(count, rows, cols):
    return [
        jax.ShapeDtypeStruct((count, cols), jnp.float32),
        jax.ShapeDtypeStruct((count, cols), jnp.float32),
        jax.ShapeDtypeStruct((count, rows), jnp.float32),
        jax.ShapeDtypeStruct((count, rows), jnp.float32),
    ]


def edges_call(flat, count, rows, cols):
    vmem = pl.BlockSpec(memory_space=pltpu.VMEM)
    return pl.pallas_call(
        functools.partial(edges_kernel, count=count, rows=rows, cols=cols),
        out_shape=edge_shapes(count, rows, cols),
        in_specs=[vmem],
        out_specs=[vmem] * 4,
    )(flat)


def substep_call(flat, above, below, left, right, vel, coupling, count, rows, cols):
    vmem = pl.BlockSpec(memory_space=pltpu.VMEM)
    return pl.pallas_call(
        functools.partial(substep_kernel, count=count, rows=rows, cols=cols),
        out_shape=[jax.ShapeDtypeStruct((count * rows, cols), jnp.float32)]
        + edge_shapes(count, rows, cols),
        in_specs=[vmem] * 7,
        out_specs=[vmem] * 5,
    )(flat, above, below, left, right, vel, coupling)


def one_substep(flat, edges, flat_velocity, coupling, count, rows, cols):
    top, bottom, first, last = edges
    above = neighbour(bottom, "gx", 1)
    below = neighbour(top, "gx", -1)
    left = neighbour(last, "gy", 1)
    right = neighbour(first, "gy", -1)
    result = substep_call(flat, above, below, left, right, flat_velocity, coupling, count, rows, cols)
    return result[0], result[1:]


def exchange_sum(array, axes, last=None):
    stages = []
    for axis in axes:
        count, stride = lax.axis_size(axis), 1
        while stride < count:
            stages.append((axis, stride))
            stride *= 2
    if last in stages:
        stages.remove(last)
        stages.append(last)
    for axis, stride in stages:
        pairs = [(i, i ^ stride) for i in range(lax.axis_size(axis))]
        array = array + lax.ppermute(array, axis, pairs)
    return array


def hdot(a, b):
    return jnp.dot(a, b, precision=lax.Precision.HIGHEST)


def inverse_kernel(a_ref, x_ref, *, size):
    sub = lax.broadcasted_iota(jnp.int32, (size, size), 0)
    lane = lax.broadcasted_iota(jnp.int32, (size, size), 1)
    lane_row = lax.broadcasted_iota(jnp.int32, (1, size), 1)
    sub_col = lax.broadcasted_iota(jnp.int32, (size, 1), 0)

    def row_at(m, k):
        return jnp.sum(jnp.where(sub == k, m, 0.0), axis=0, keepdims=True)

    def col_at(m, k):
        return jnp.sum(jnp.where(lane == k, m, 0.0), axis=1, keepdims=True)

    def lane_at(v, k):
        return jnp.sum(jnp.where(lane_row == k, v, 0.0), axis=1, keepdims=True)

    def step(k, carry):
        a, x, row, col, x_raw = carry
        scale = 1.0 / jnp.sqrt(lane_at(row, k))
        cross = lane_at(row, k + 1) * scale
        low_row = jnp.where(lane_row >= k, row, 0.0) * scale
        low_col = jnp.where(sub_col >= k, col, 0.0) * scale
        x_row = x_raw * scale
        next_row = row_at(a, k + 1) - cross * low_row
        next_col = col_at(a, k + 1) - cross * low_col
        next_x = row_at(x, k + 1) - cross * x_row
        a = a - low_col * low_row
        x = jnp.where(sub == k, x_row, x - jnp.where(sub_col > k, low_col, 0.0) * x_row)
        return a, x, next_row, next_col, next_x

    a0 = a_ref[...]
    eye = jnp.where(sub == lane, 1.0, 0.0).astype(jnp.float32)
    init = (a0, eye, row_at(a0, 0), col_at(a0, 0), row_at(eye, 0))
    x = lax.fori_loop(0, size, step, init, unroll=4)[1]
    x_ref[...] = x


def lower_inverse_call(matrix):
    size = matrix.shape[0]
    vmem = pl.BlockSpec(memory_space=pltpu.VMEM)
    return pl.pallas_call(
        functools.partial(inverse_kernel, size=size),
        out_shape=jax.ShapeDtypeStruct((size, size), jnp.float32),
        in_specs=[vmem],
        out_specs=vmem,
    )(matrix)

def lower_inverse(matrix):
    return lower_inverse_call(0.5 * (matrix + matrix.T))


def body(basis_fields, carried_fields, velocity, diffusion, advection):
    basis_rank, tile_rows, tile_cols = carried_fields.shape
    tile_cells = tile_rows * tile_cols
    aug_count = 2 * basis_rank
    cell_weight = 1.0 / (tile_cells * lax.axis_size("gx") * lax.axis_size("gy"))
    axes = ("gy", "gx")
    flat_basis = basis_fields.reshape(basis_rank, tile_cells)
    flat_carried = carried_fields.reshape(basis_rank, tile_cells)
    known = jnp.concatenate([flat_basis, flat_carried], 0)
    basis_sum = exchange_sum(hdot(flat_basis, known.T), axes) * cell_weight
    flat_velocity = velocity.reshape(2 * tile_rows, tile_cols)
    coupling = jnp.concatenate([diffusion.T, -advection.T], 1)
    shape = (basis_rank, tile_rows, tile_cols)
    carried_rows = carried_fields.reshape(basis_rank * tile_rows, tile_cols)
    edges = edges_call(carried_rows, *shape)
    section_one, edges = one_substep(carried_rows, edges, flat_velocity, coupling, *shape)
    section_two, _ = one_substep(section_one, edges, flat_velocity, coupling, *shape)
    flat_new = section_two.reshape(basis_rank, tile_cells)
    every = jnp.concatenate([flat_basis, flat_new, flat_carried], 0)
    new_sum = exchange_sum(hdot(flat_new, every.T), axes, last=("gy", 1)) * cell_weight
    inverse_11 = lower_inverse(basis_sum[:, :basis_rank])
    low_21 = hdot(new_sum[:, :basis_rank], inverse_11.T)
    schur = new_sum[:, basis_rank:aug_count] - hdot(low_21, low_21.T)
    inverse_22 = lower_inverse(schur)
    top = hdot(inverse_11, flat_basis)
    bottom = hdot(inverse_22, flat_new - hdot(low_21, top))
    new_basis = jnp.concatenate([top, bottom], 0)
    galerkin_top = hdot(inverse_11, basis_sum[:, basis_rank:])
    galerkin_bottom = hdot(inverse_22, new_sum[:, aug_count:] - hdot(low_21, galerkin_top))
    galerkin = jnp.concatenate([galerkin_top, galerkin_bottom], 0)
    return (new_basis.reshape(aug_count, tile_rows, tile_cols), galerkin)


def solution(mesh):
    in_specs = (P(None, "gx", "gy"), P(None, "gx", "gy"), P(None, "gx", "gy"), P(), P())
    out_specs = (P(None, "gx", "gy"), P())
    return jax.shard_map(body, mesh=mesh, in_specs=in_specs, out_specs=out_specs, check_vma=False)
```

```python
import functools
import jax
import jax.numpy as jnp
from jax import lax
from jax.experimental import pallas as pl
from jax.experimental.pallas import tpu as pltpu
from jax.sharding import PartitionSpec as P


def neighbour(array, axis, step):
    count = lax.axis_size(axis)
    pairs = [(i, (i + step) % count) for i in range(count)]
    return lax.ppermute(array, axis, pairs)


def keep_edges(r, block, top_ref, bottom_ref, first_ref, last_ref, rows, cols):
    if r == 0:
        top_ref[...] = block
    if r == rows - 1:
        bottom_ref[...] = block
    first_ref[:, r:r + 1] = block[:, 0:1]
    last_ref[:, r:r + 1] = block[:, cols - 1:cols]


def edges_kernel(f_ref, top_ref, bottom_ref, first_ref, last_ref, *, count, rows, cols):
    for r in range(rows):
        block = f_ref[pl.ds(r, count, stride=rows), :]
        keep_edges(r, block, top_ref, bottom_ref, first_ref, last_ref, rows, cols)


def substep_kernel(f_ref, above_ref, below_ref, left_ref, right_ref, vel_ref, mix_ref, out_ref,
                   top_ref, bottom_ref, first_ref, last_ref, *, count, rows, cols):
    col_id = lax.broadcasted_iota(jnp.int32, (count, cols), 1)
    row_lane = lax.broadcasted_iota(jnp.int32, (count, rows), 1)
    coupling = mix_ref[...]

    def grid_row(r):
        return f_ref[pl.ds(r, count, stride=rows), :]

    def one_row(r, prev, here, nxt):
        pick = row_lane == r
        west = jnp.sum(jnp.where(pick, left_ref[...], 0.0), axis=1, keepdims=True)
        east = jnp.sum(jnp.where(pick, right_ref[...], 0.0), axis=1, keepdims=True)
        minus_y = jnp.where(col_id == 0, west, pltpu.roll(here, 1, 1))
        plus_y = jnp.where(col_id == cols - 1, east, pltpu.roll(here, cols - 1, 1))
        speed_x = vel_ref[pl.ds(r, 1), :]
        speed_y = vel_ref[pl.ds(rows + r, 1), :]
        laplace = nxt + prev + plus_y + minus_y - 4.0 * here
        transport = speed_x * (nxt - prev) * 0.5 + speed_y * (plus_y - minus_y) * 0.5
        rate = jnp.dot(coupling, jnp.concatenate([laplace, transport], 0),
                       precision=lax.Precision.HIGHEST, preferred_element_type=jnp.float32)
        result = here + rate
        out_ref[pl.ds(r, count, stride=rows), :] = result
        return result

    def keep_columns(r, result, firsts, lasts):
        pick = row_lane == r
        firsts = jnp.where(pick, result[:, 0:1], firsts)
        lasts = jnp.where(pick, result[:, cols - 1:cols], lasts)
        return firsts, lasts

    empty = jnp.zeros((count, rows), jnp.float32)
    result = one_row(0, above_ref[...], grid_row(0), grid_row(1))
    top_ref[...] = result
    firsts, lasts = keep_columns(0, result, empty, empty)

    def middle(r, carry):
        result = one_row(r, grid_row(r - 1), grid_row(r), grid_row(r + 1))
        return keep_columns(r, result, *carry)

    firsts, lasts = lax.fori_loop(1, rows - 1, middle, (firsts, lasts))
    result = one_row(rows - 1, grid_row(rows - 2), grid_row(rows - 1), below_ref[...])
    bottom_ref[...] = result
    firsts, lasts = keep_columns(rows - 1, result, firsts, lasts)
    first_ref[...] = firsts
    last_ref[...] = lasts


def edge_shapes(count, rows, cols):
    return [
        jax.ShapeDtypeStruct((count, cols), jnp.float32),
        jax.ShapeDtypeStruct((count, cols), jnp.float32),
        jax.ShapeDtypeStruct((count, rows), jnp.float32),
        jax.ShapeDtypeStruct((count, rows), jnp.float32),
    ]


def edges_call(flat, count, rows, cols):
    vmem = pl.BlockSpec(memory_space=pltpu.VMEM)
    return pl.pallas_call(
        functools.partial(edges_kernel, count=count, rows=rows, cols=cols),
        out_shape=edge_shapes(count, rows, cols),
        in_specs=[vmem],
        out_specs=[vmem] * 4,
    )(flat)


def substep_call(flat, above, below, left, right, vel, coupling, count, rows, cols):
    vmem = pl.BlockSpec(memory_space=pltpu.VMEM)
    return pl.pallas_call(
        functools.partial(substep_kernel, count=count, rows=rows, cols=cols),
        out_shape=[jax.ShapeDtypeStruct((count * rows, cols), jnp.float32)]
        + edge_shapes(count, rows, cols),
        in_specs=[vmem] * 7,
        out_specs=[vmem] * 5,
    )(flat, above, below, left, right, vel, coupling)


def one_substep(flat, edges, flat_velocity, coupling, count, rows, cols):
    top, bottom, first, last = edges
    above = neighbour(bottom, "gx", 1)
    below = neighbour(top, "gx", -1)
    left = neighbour(last, "gy", 1)
    right = neighbour(first, "gy", -1)
    result = substep_call(flat, above, below, left, right, flat_velocity, coupling, count, rows, cols)
    return result[0], result[1:]


def exchange_sum(array, axes, last=None):
    stages = []
    for axis in axes:
        count, stride = lax.axis_size(axis), 1
        while stride < count:
            stages.append((axis, stride))
            stride *= 2
    if last in stages:
        stages.remove(last)
        stages.append(last)
    for axis, stride in stages:
        pairs = [(i, i ^ stride) for i in range(lax.axis_size(axis))]
        array = array + lax.ppermute(array, axis, pairs)
    return array


def hdot(a, b):
    return jnp.dot(a, b, precision=lax.Precision.HIGHEST)


def inverse_kernel(a_ref, x_ref, *, size):
    sub = lax.broadcasted_iota(jnp.int32, (size, size), 0)
    lane = lax.broadcasted_iota(jnp.int32, (size, size), 1)
    lane_row = lax.broadcasted_iota(jnp.int32, (1, size), 1)
    sub_col = lax.broadcasted_iota(jnp.int32, (size, 1), 0)

    def row_at(m, k):
        return jnp.sum(jnp.where(sub == k, m, 0.0), axis=0, keepdims=True)

    def col_at(m, k):
        return jnp.sum(jnp.where(lane == k, m, 0.0), axis=1, keepdims=True)

    def lane_at(v, k):
        return jnp.sum(jnp.where(lane_row == k, v, 0.0), axis=1, keepdims=True)

    def step(k, carry):
        a, x, row, col, x_raw = carry
        scale = 1.0 / jnp.sqrt(lane_at(row, k))
        cross = lane_at(row, k + 1) * scale
        low_row = jnp.where(lane_row >= k, row, 0.0) * scale
        low_col = jnp.where(sub_col >= k, col, 0.0) * scale
        x_row = x_raw * scale
        next_row = row_at(a, k + 1) - cross * low_row
        next_col = col_at(a, k + 1) - cross * low_col
        next_x = row_at(x, k + 1) - cross * x_row
        a = a - low_col * low_row
        x = jnp.where(sub == k, x_row, x - jnp.where(sub_col > k, low_col, 0.0) * x_row)
        return a, x, next_row, next_col, next_x

    a0 = a_ref[...]
    eye = jnp.where(sub == lane, 1.0, 0.0).astype(jnp.float32)
    init = (a0, eye, row_at(a0, 0), col_at(a0, 0), row_at(eye, 0))
    x = lax.fori_loop(0, size, step, init, unroll=4)[1]
    x_ref[...] = x


def lower_inverse_call(matrix):
    size = matrix.shape[0]
    vmem = pl.BlockSpec(memory_space=pltpu.VMEM)
    return pl.pallas_call(
        functools.partial(inverse_kernel, size=size),
        out_shape=jax.ShapeDtypeStruct((size, size), jnp.float32),
        in_specs=[vmem],
        out_specs=vmem,
    )(matrix)

def lower_inverse(matrix):
    return lower_inverse_call(0.5 * (matrix + matrix.T))


def body(basis_fields, carried_fields, velocity, diffusion, advection):
    basis_rank, tile_rows, tile_cols = carried_fields.shape
    tile_cells = tile_rows * tile_cols
    aug_count = 2 * basis_rank
    cell_weight = 1.0 / (tile_cells * lax.axis_size("gx") * lax.axis_size("gy"))
    axes = ("gy", "gx")
    flat_basis = basis_fields.reshape(basis_rank, tile_cells)
    flat_carried = carried_fields.reshape(basis_rank, tile_cells)
    known = jnp.concatenate([flat_basis, flat_carried], 0)
    basis_sum = exchange_sum(hdot(flat_basis, known.T), axes) * cell_weight
    flat_velocity = velocity.reshape(2 * tile_rows, tile_cols)
    coupling = jnp.concatenate([diffusion.T, -advection.T], 1)
    shape = (basis_rank, tile_rows, tile_cols)
    carried_rows = carried_fields.reshape(basis_rank * tile_rows, tile_cols)
    edges = edges_call(carried_rows, *shape)
    section_one, edges = one_substep(carried_rows, edges, flat_velocity, coupling, *shape)
    section_two, _ = one_substep(section_one, edges, flat_velocity, coupling, *shape)
    flat_new = section_two.reshape(basis_rank, tile_cells)
    every = jnp.concatenate([flat_basis, flat_new, flat_carried], 0)
    new_sum = exchange_sum(hdot(flat_new, every.T), axes, last=("gy", 1)) * cell_weight
    inverse_11 = lower_inverse(basis_sum[:, :basis_rank])
    low_21 = hdot(new_sum[:, :basis_rank], inverse_11.T)
    schur = new_sum[:, basis_rank:aug_count] - hdot(low_21, low_21.T)
    inverse_22 = lower_inverse(schur)
    top = hdot(inverse_11, flat_basis)
    bottom = hdot(inverse_22, flat_new - hdot(low_21, top))
    new_basis = jnp.concatenate([top, bottom], 0)
    galerkin_top = hdot(inverse_11, basis_sum[:, basis_rank:])
    galerkin_bottom = hdot(inverse_22, new_sum[:, aug_count:] - hdot(low_21, galerkin_top))
    galerkin = jnp.concatenate([galerkin_top, galerkin_bottom], 0)
    return (new_basis.reshape(aug_count, tile_rows, tile_cols), galerkin)


def solution(mesh):
    in_specs = (P(None, "gx", "gy"), P(None, "gx", "gy"), P(None, "gx", "gy"), P(), P())
    out_specs = (P(None, "gx", "gy"), P())
    return jax.shard_map(body, mesh=mesh, in_specs=in_specs, out_specs=out_specs, check_vma=False)
```

```python
import functools
import jax
import jax.numpy as jnp
from jax import lax
from jax.experimental import pallas as pl
from jax.experimental.pallas import tpu as pltpu
from jax.sharding import PartitionSpec as P


def neighbour(array, axis, step):
    count = lax.axis_size(axis)
    pairs = [(i, (i + step) % count) for i in range(count)]
    return lax.ppermute(array, axis, pairs)


def keep_edges(r, block, top_ref, bottom_ref, first_ref, last_ref, rows, cols):
    if r == 0:
        top_ref[...] = block
    if r == rows - 1:
        bottom_ref[...] = block
    first_ref[:, r:r + 1] = block[:, 0:1]
    last_ref[:, r:r + 1] = block[:, cols - 1:cols]


def edges_kernel(f_ref, top_ref, bottom_ref, first_ref, last_ref, *, count, rows, cols):
    for r in range(rows):
        block = f_ref[pl.ds(r, count, stride=rows), :]
        keep_edges(r, block, top_ref, bottom_ref, first_ref, last_ref, rows, cols)


def substep_kernel(f_ref, above_ref, below_ref, left_ref, right_ref, vel_ref, mix_ref, out_ref,
                   top_ref, bottom_ref, first_ref, last_ref, *, count, rows, cols):
    col_id = lax.broadcasted_iota(jnp.int32, (count, cols), 1)
    coupling = mix_ref[...]

    def row_of(r):
        if r < 0:
            return above_ref[...]
        if r >= rows:
            return below_ref[...]
        return f_ref[pl.ds(r, count, stride=rows), :]

    prev, here = row_of(-1), row_of(0)
    for r in range(rows):
        nxt = row_of(r + 1)
        west = left_ref[:, r:r + 1]
        east = right_ref[:, r:r + 1]
        minus_y = jnp.where(col_id == 0, west, pltpu.roll(here, 1, 1))
        plus_y = jnp.where(col_id == cols - 1, east, pltpu.roll(here, cols - 1, 1))
        speed_x = vel_ref[r:r + 1, :]
        speed_y = vel_ref[rows + r:rows + r + 1, :]
        laplace = nxt + prev + plus_y + minus_y - 4.0 * here
        transport = speed_x * (nxt - prev) * 0.5 + speed_y * (plus_y - minus_y) * 0.5
        rate = jnp.dot(coupling, jnp.concatenate([laplace, transport], 0),
                       precision=lax.Precision.HIGHEST, preferred_element_type=jnp.float32)
        result = here + rate
        out_ref[pl.ds(r, count, stride=rows), :] = result
        keep_edges(r, result, top_ref, bottom_ref, first_ref, last_ref, rows, cols)
        prev, here = here, nxt


def edge_shapes(count, rows, cols):
    return [
        jax.ShapeDtypeStruct((count, cols), jnp.float32),
        jax.ShapeDtypeStruct((count, cols), jnp.float32),
        jax.ShapeDtypeStruct((count, rows), jnp.float32),
        jax.ShapeDtypeStruct((count, rows), jnp.float32),
    ]


def edges_call(flat, count, rows, cols):
    vmem = pl.BlockSpec(memory_space=pltpu.VMEM)
    return pl.pallas_call(
        functools.partial(edges_kernel, count=count, rows=rows, cols=cols),
        out_shape=edge_shapes(count, rows, cols),
        in_specs=[vmem],
        out_specs=[vmem] * 4,
    )(flat)


def substep_call(flat, above, below, left, right, vel, coupling, count, rows, cols):
    vmem = pl.BlockSpec(memory_space=pltpu.VMEM)
    return pl.pallas_call(
        functools.partial(substep_kernel, count=count, rows=rows, cols=cols),
        out_shape=[jax.ShapeDtypeStruct((count * rows, cols), jnp.float32)]
        + edge_shapes(count, rows, cols),
        in_specs=[vmem] * 7,
        out_specs=[vmem] * 5,
    )(flat, above, below, left, right, vel, coupling)


def one_substep(flat, edges, flat_velocity, coupling, count, rows, cols):
    top, bottom, first, last = edges
    above = neighbour(bottom, "gx", 1)
    below = neighbour(top, "gx", -1)
    left = neighbour(last, "gy", 1)
    right = neighbour(first, "gy", -1)
    result = substep_call(flat, above, below, left, right, flat_velocity, coupling, count, rows, cols)
    return result[0], result[1:]


def exchange_sum(array, axes, last=None, hold=None):
    stages = []
    for axis in axes:
        count, stride = lax.axis_size(axis), 1
        while stride < count:
            stages.append((axis, stride))
            stride *= 2
    if last in stages:
        stages.remove(last)
        stages.append(last)
    for number, (axis, stride) in enumerate(stages):
        if number == 1 and hold is not None:
            array, hold = lax.optimization_barrier((array, hold))
        pairs = [(i, i ^ stride) for i in range(lax.axis_size(axis))]
        array = array + lax.ppermute(array, axis, pairs)
    return array if hold is None else (array, hold)


def hdot(a, b):
    return jnp.dot(a, b, precision=lax.Precision.HIGHEST)


def inverse_kernel(a_ref, x_ref, *, size):
    sub = lax.broadcasted_iota(jnp.int32, (size, size), 0)
    lane = lax.broadcasted_iota(jnp.int32, (size, size), 1)
    lane_row = lax.broadcasted_iota(jnp.int32, (1, size), 1)
    sub_col = lax.broadcasted_iota(jnp.int32, (size, 1), 0)

    def row_at(m, k):
        return jnp.sum(jnp.where(sub == k, m, 0.0), axis=0, keepdims=True)

    def col_at(m, k):
        return jnp.sum(jnp.where(lane == k, m, 0.0), axis=1, keepdims=True)

    def lane_at(v, k):
        return jnp.sum(jnp.where(lane_row == k, v, 0.0), axis=1, keepdims=True)

    def step(k, carry):
        a, x, row, col, x_raw = carry
        scale = 1.0 / jnp.sqrt(lane_at(row, k))
        cross = lane_at(row, k + 1) * scale
        low_row = jnp.where(lane_row >= k, row, 0.0) * scale
        low_col = jnp.where(sub_col >= k, col, 0.0) * scale
        x_row = x_raw * scale
        next_row = row_at(a, k + 1) - cross * low_row
        next_col = col_at(a, k + 1) - cross * low_col
        next_x = row_at(x, k + 1) - cross * x_row
        a = a - low_col * low_row
        x = jnp.where(sub == k, x_row, x - jnp.where(sub_col > k, low_col, 0.0) * x_row)
        return a, x, next_row, next_col, next_x

    a0 = a_ref[...]
    eye = jnp.where(sub == lane, 1.0, 0.0).astype(jnp.float32)
    init = (a0, eye, row_at(a0, 0), col_at(a0, 0), row_at(eye, 0))
    x = lax.fori_loop(0, size, step, init, unroll=4)[1]
    x_ref[...] = x


def lower_inverse_call(matrix):
    size = matrix.shape[0]
    vmem = pl.BlockSpec(memory_space=pltpu.VMEM)
    return pl.pallas_call(
        functools.partial(inverse_kernel, size=size),
        out_shape=jax.ShapeDtypeStruct((size, size), jnp.float32),
        in_specs=[vmem],
        out_specs=vmem,
    )(matrix)

def lower_inverse(matrix):
    return lower_inverse_call(0.5 * (matrix + matrix.T))


def body(basis_fields, carried_fields, velocity, diffusion, advection):
    basis_rank, tile_rows, tile_cols = carried_fields.shape
    tile_cells = tile_rows * tile_cols
    aug_count = 2 * basis_rank
    cell_weight = 1.0 / (tile_cells * lax.axis_size("gx") * lax.axis_size("gy"))
    axes = ("gy", "gx")
    flat_basis = basis_fields.reshape(basis_rank, tile_cells)
    flat_carried = carried_fields.reshape(basis_rank, tile_cells)
    known = jnp.concatenate([flat_basis, flat_carried], 0)
    basis_sum = exchange_sum(hdot(flat_basis, known.T), axes) * cell_weight
    flat_velocity = velocity.reshape(2 * tile_rows, tile_cols)
    coupling = jnp.concatenate([diffusion.T, -advection.T], 1)
    shape = (basis_rank, tile_rows, tile_cols)
    carried_rows = carried_fields.reshape(basis_rank * tile_rows, tile_cols)
    edges = edges_call(carried_rows, *shape)
    section_one, edges = one_substep(carried_rows, edges, flat_velocity, coupling, *shape)
    section_two, _ = one_substep(section_one, edges, flat_velocity, coupling, *shape)
    flat_new = section_two.reshape(basis_rank, tile_cells)
    every = jnp.concatenate([flat_basis, flat_new, flat_carried], 0)
    inverse_11 = lower_inverse(basis_sum[:, :basis_rank])
    new_sum, inverse_11 = exchange_sum(
        hdot(flat_new, every.T), axes, last=("gy", 1), hold=inverse_11
    )
    new_sum = new_sum * cell_weight
    low_21 = hdot(new_sum[:, :basis_rank], inverse_11.T)
    schur = new_sum[:, basis_rank:aug_count] - hdot(low_21, low_21.T)
    inverse_22 = lower_inverse(schur)
    top = hdot(inverse_11, flat_basis)
    bottom = hdot(inverse_22, flat_new - hdot(low_21, top))
    new_basis = jnp.concatenate([top, bottom], 0)
    galerkin_top = hdot(inverse_11, basis_sum[:, basis_rank:])
    galerkin_bottom = hdot(inverse_22, new_sum[:, aug_count:] - hdot(low_21, galerkin_top))
    galerkin = jnp.concatenate([galerkin_top, galerkin_bottom], 0)
    return (new_basis.reshape(aug_count, tile_rows, tile_cols), galerkin)


def solution(mesh):
    in_specs = (P(None, "gx", "gy"), P(None, "gx", "gy"), P(None, "gx", "gy"), P(), P())
    out_specs = (P(None, "gx", "gy"), P())
    return jax.shard_map(body, mesh=mesh, in_specs=in_specs, out_specs=out_specs, check_vma=False)
```

```python
import functools
import jax
import jax.numpy as jnp
from jax import lax
from jax.experimental import pallas as pl
from jax.experimental.pallas import tpu as pltpu
from jax.sharding import PartitionSpec as P


def neighbour(array, axis, step):
    count = lax.axis_size(axis)
    pairs = [(i, (i + step) % count) for i in range(count)]
    return lax.ppermute(array, axis, pairs)


def keep_edges(r, block, top_ref, bottom_ref, first_ref, last_ref, rows, cols):
    if r == 0:
        top_ref[...] = block
    if r == rows - 1:
        bottom_ref[...] = block
    first_ref[:, r:r + 1] = block[:, 0:1]
    last_ref[:, r:r + 1] = block[:, cols - 1:cols]


def edges_kernel(f_ref, top_ref, bottom_ref, first_ref, last_ref, *, count, rows, cols):
    for r in range(rows):
        block = f_ref[pl.ds(r, count, stride=rows), :]
        keep_edges(r, block, top_ref, bottom_ref, first_ref, last_ref, rows, cols)


def substep_kernel(f_ref, above_ref, below_ref, left_ref, right_ref, vel_ref, mix_ref, out_ref,
                   top_ref, bottom_ref, first_ref, last_ref, *, count, rows, cols):
    col_id = lax.broadcasted_iota(jnp.int32, (count, cols), 1)
    coupling = mix_ref[...]

    def row_of(r):
        if r < 0:
            return above_ref[...]
        if r >= rows:
            return below_ref[...]
        return f_ref[pl.ds(r, count, stride=rows), :]

    prev, here = row_of(-1), row_of(0)
    for r in range(rows):
        nxt = row_of(r + 1)
        west = left_ref[:, r:r + 1]
        east = right_ref[:, r:r + 1]
        minus_y = jnp.where(col_id == 0, west, pltpu.roll(here, 1, 1))
        plus_y = jnp.where(col_id == cols - 1, east, pltpu.roll(here, cols - 1, 1))
        speed_x = vel_ref[r:r + 1, :]
        speed_y = vel_ref[rows + r:rows + r + 1, :]
        laplace = nxt + prev + plus_y + minus_y - 4.0 * here
        transport = speed_x * (nxt - prev) * 0.5 + speed_y * (plus_y - minus_y) * 0.5
        rate = jnp.dot(coupling, jnp.concatenate([laplace, transport], 0),
                       precision=lax.Precision.HIGHEST, preferred_element_type=jnp.float32)
        result = here + rate
        out_ref[pl.ds(r, count, stride=rows), :] = result
        keep_edges(r, result, top_ref, bottom_ref, first_ref, last_ref, rows, cols)
        prev, here = here, nxt


def edge_shapes(count, rows, cols):
    return [
        jax.ShapeDtypeStruct((count, cols), jnp.float32),
        jax.ShapeDtypeStruct((count, cols), jnp.float32),
        jax.ShapeDtypeStruct((count, rows), jnp.float32),
        jax.ShapeDtypeStruct((count, rows), jnp.float32),
    ]


def edges_call(flat, count, rows, cols):
    vmem = pl.BlockSpec(memory_space=pltpu.VMEM)
    return pl.pallas_call(
        functools.partial(edges_kernel, count=count, rows=rows, cols=cols),
        out_shape=edge_shapes(count, rows, cols),
        in_specs=[vmem],
        out_specs=[vmem] * 4,
    )(flat)


def substep_call(flat, above, below, left, right, vel, coupling, count, rows, cols):
    vmem = pl.BlockSpec(memory_space=pltpu.VMEM)
    return pl.pallas_call(
        functools.partial(substep_kernel, count=count, rows=rows, cols=cols),
        out_shape=[jax.ShapeDtypeStruct((count * rows, cols), jnp.float32)]
        + edge_shapes(count, rows, cols),
        in_specs=[vmem] * 7,
        out_specs=[vmem] * 5,
    )(flat, above, below, left, right, vel, coupling)


def one_substep(flat, edges, flat_velocity, coupling, count, rows, cols):
    top, bottom, first, last = edges
    above = neighbour(bottom, "gx", 1)
    below = neighbour(top, "gx", -1)
    left = neighbour(last, "gy", 1)
    right = neighbour(first, "gy", -1)
    result = substep_call(flat, above, below, left, right, flat_velocity, coupling, count, rows, cols)
    return result[0], result[1:]


def exchange_sum(array, axes, last=None):
    stages = []
    for axis in axes:
        count, stride = lax.axis_size(axis), 1
        while stride < count:
            stages.append((axis, stride))
            stride *= 2
    if last in stages:
        stages.remove(last)
        stages.append(last)
    for axis, stride in stages:
        pairs = [(i, i ^ stride) for i in range(lax.axis_size(axis))]
        array = array + lax.ppermute(array, axis, pairs)
    return array


def hdot(a, b):
    return jnp.dot(a, b, precision=lax.Precision.HIGHEST)


def inverse_kernel(a_ref, x_ref, *, size):
    sub = lax.broadcasted_iota(jnp.int32, (size, size), 0)
    lane = lax.broadcasted_iota(jnp.int32, (size, size), 1)
    lane_row = lax.broadcasted_iota(jnp.int32, (1, size), 1)
    sub_col = lax.broadcasted_iota(jnp.int32, (size, 1), 0)

    def row_at(m, k):
        return jnp.sum(jnp.where(sub == k, m, 0.0), axis=0, keepdims=True)

    def col_at(m, k):
        return jnp.sum(jnp.where(lane == k, m, 0.0), axis=1, keepdims=True)

    def lane_at(v, k):
        return jnp.sum(jnp.where(lane_row == k, v, 0.0), axis=1, keepdims=True)

    def step(k, carry):
        a, x, row, col, x_raw = carry
        scale = 1.0 / jnp.sqrt(lane_at(row, k))
        cross = lane_at(row, k + 1) * scale
        low_row = jnp.where(lane_row >= k, row, 0.0) * scale
        low_col = jnp.where(sub_col >= k, col, 0.0) * scale
        x_row = x_raw * scale
        next_row = row_at(a, k + 1) - cross * low_row
        next_col = col_at(a, k + 1) - cross * low_col
        next_x = row_at(x, k + 1) - cross * x_row
        a = a - low_col * low_row
        x = jnp.where(sub == k, x_row, x - jnp.where(sub_col > k, low_col, 0.0) * x_row)
        return a, x, next_row, next_col, next_x

    a0 = a_ref[...]
    eye = jnp.where(sub == lane, 1.0, 0.0).astype(jnp.float32)
    init = (a0, eye, row_at(a0, 0), col_at(a0, 0), row_at(eye, 0))
    x = lax.fori_loop(0, size, step, init, unroll=4)[1]
    x_ref[...] = x


def lower_inverse_call(matrix):
    size = matrix.shape[0]
    vmem = pl.BlockSpec(memory_space=pltpu.VMEM)
    return pl.pallas_call(
        functools.partial(inverse_kernel, size=size),
        out_shape=jax.ShapeDtypeStruct((size, size), jnp.float32),
        in_specs=[vmem],
        out_specs=vmem,
    )(matrix)

def lower_inverse(matrix):
    return lower_inverse_call(0.5 * (matrix + matrix.T))


def body(basis_fields, carried_fields, velocity, diffusion, advection):
    basis_rank, tile_rows, tile_cols = carried_fields.shape
    tile_cells = tile_rows * tile_cols
    aug_count = 2 * basis_rank
    cell_weight = 1.0 / (tile_cells * lax.axis_size("gx") * lax.axis_size("gy"))
    axes = ("gy", "gx")
    flat_basis = basis_fields.reshape(basis_rank, tile_cells)
    flat_carried = carried_fields.reshape(basis_rank, tile_cells)
    known = jnp.concatenate([flat_basis, flat_carried], 0)
    basis_sum = exchange_sum(hdot(flat_basis, known.T), axes) * cell_weight
    flat_velocity = velocity.reshape(2 * tile_rows, tile_cols)
    coupling = jnp.concatenate([diffusion.T, -advection.T], 1)
    shape = (basis_rank, tile_rows, tile_cols)
    carried_rows = carried_fields.reshape(basis_rank * tile_rows, tile_cols)
    edges = edges_call(carried_rows, *shape)
    section_one, edges = one_substep(carried_rows, edges, flat_velocity, coupling, *shape)
    section_two, _ = one_substep(section_one, edges, flat_velocity, coupling, *shape)
    flat_new = section_two.reshape(basis_rank, tile_cells)
    new_rows = section_two.reshape(shape)
    every = jnp.concatenate([basis_fields, new_rows, carried_fields], 0)
    new_part = lax.dot_general(new_rows, every, (((1, 2), (1, 2)), ((), ())),
                               precision=lax.Precision.HIGHEST)
    new_sum = exchange_sum(new_part, axes, last=("gy", 1)) * cell_weight
    inverse_11 = lower_inverse(basis_sum[:, :basis_rank])
    low_21 = hdot(new_sum[:, :basis_rank], inverse_11.T)
    schur = new_sum[:, basis_rank:aug_count] - hdot(low_21, low_21.T)
    inverse_22 = lower_inverse(schur)
    top = hdot(inverse_11, flat_basis)
    bottom = hdot(inverse_22, flat_new - hdot(low_21, top))
    new_basis = jnp.concatenate([top, bottom], 0)
    galerkin_top = hdot(inverse_11, basis_sum[:, basis_rank:])
    galerkin_bottom = hdot(inverse_22, new_sum[:, aug_count:] - hdot(low_21, galerkin_top))
    galerkin = jnp.concatenate([galerkin_top, galerkin_bottom], 0)
    return (new_basis.reshape(aug_count, tile_rows, tile_cols), galerkin)


def solution(mesh):
    in_specs = (P(None, "gx", "gy"), P(None, "gx", "gy"), P(None, "gx", "gy"), P(), P())
    out_specs = (P(None, "gx", "gy"), P())
    return jax.shard_map(body, mesh=mesh, in_specs=in_specs, out_specs=out_specs, check_vma=False)
```

```python
import functools
import jax
import jax.numpy as jnp
from jax import lax
from jax.experimental import pallas as pl
from jax.experimental.pallas import tpu as pltpu
from jax.sharding import PartitionSpec as P


def neighbour(array, axis, step):
    count = lax.axis_size(axis)
    pairs = [(i, (i + step) % count) for i in range(count)]
    return lax.ppermute(array, axis, pairs)


def keep_edges(r, block, top_ref, bottom_ref, first_ref, last_ref, rows, cols):
    if r == 0:
        top_ref[...] = block
    if r == rows - 1:
        bottom_ref[...] = block
    first_ref[:, r:r + 1] = block[:, 0:1]
    last_ref[:, r:r + 1] = block[:, cols - 1:cols]


def edges_kernel(f_ref, top_ref, bottom_ref, first_ref, last_ref, *, count, rows, cols):
    row_lane = lax.broadcasted_iota(jnp.int32, (count, rows), 1)
    firsts = jnp.zeros((count, rows), jnp.float32)
    lasts = jnp.zeros((count, rows), jnp.float32)
    for r in range(rows):
        block = f_ref[pl.ds(r, count, stride=rows), :]
        if r == 0:
            top_ref[...] = block
        if r == rows - 1:
            bottom_ref[...] = block
        firsts = jnp.where(row_lane == r, block[:, 0:1], firsts)
        lasts = jnp.where(row_lane == r, block[:, cols - 1:cols], lasts)
    first_ref[...] = firsts
    last_ref[...] = lasts


def substep_kernel(f_ref, above_ref, below_ref, left_ref, right_ref, vel_ref, mix_ref, out_ref,
                   top_ref, bottom_ref, first_ref, last_ref, *, count, rows, cols):
    col_id = lax.broadcasted_iota(jnp.int32, (count, cols), 1)
    coupling = mix_ref[...]

    def row_of(r):
        if r < 0:
            return above_ref[...]
        if r >= rows:
            return below_ref[...]
        return f_ref[pl.ds(r, count, stride=rows), :]

    prev, here = row_of(-1), row_of(0)
    for r in range(rows):
        nxt = row_of(r + 1)
        west = left_ref[:, r:r + 1]
        east = right_ref[:, r:r + 1]
        minus_y = jnp.where(col_id == 0, west, pltpu.roll(here, 1, 1))
        plus_y = jnp.where(col_id == cols - 1, east, pltpu.roll(here, cols - 1, 1))
        speed_x = vel_ref[r:r + 1, :]
        speed_y = vel_ref[rows + r:rows + r + 1, :]
        laplace = nxt + prev + plus_y + minus_y - 4.0 * here
        transport = speed_x * (nxt - prev) * 0.5 + speed_y * (plus_y - minus_y) * 0.5
        rate = jnp.dot(coupling, jnp.concatenate([laplace, transport], 0),
                       precision=lax.Precision.HIGHEST, preferred_element_type=jnp.float32)
        result = here + rate
        out_ref[pl.ds(r, count, stride=rows), :] = result
        keep_edges(r, result, top_ref, bottom_ref, first_ref, last_ref, rows, cols)
        prev, here = here, nxt


def edge_shapes(count, rows, cols):
    return [
        jax.ShapeDtypeStruct((count, cols), jnp.float32),
        jax.ShapeDtypeStruct((count, cols), jnp.float32),
        jax.ShapeDtypeStruct((count, rows), jnp.float32),
        jax.ShapeDtypeStruct((count, rows), jnp.float32),
    ]


def edges_call(flat, count, rows, cols):
    vmem = pl.BlockSpec(memory_space=pltpu.VMEM)
    return pl.pallas_call(
        functools.partial(edges_kernel, count=count, rows=rows, cols=cols),
        out_shape=edge_shapes(count, rows, cols),
        in_specs=[vmem],
        out_specs=[vmem] * 4,
    )(flat)


def substep_call(flat, above, below, left, right, vel, coupling, count, rows, cols):
    vmem = pl.BlockSpec(memory_space=pltpu.VMEM)
    return pl.pallas_call(
        functools.partial(substep_kernel, count=count, rows=rows, cols=cols),
        out_shape=[jax.ShapeDtypeStruct((count * rows, cols), jnp.float32)]
        + edge_shapes(count, rows, cols),
        in_specs=[vmem] * 7,
        out_specs=[vmem] * 5,
    )(flat, above, below, left, right, vel, coupling)


def one_substep(flat, edges, flat_velocity, coupling, count, rows, cols):
    top, bottom, first, last = edges
    above = neighbour(bottom, "gx", 1)
    below = neighbour(top, "gx", -1)
    left = neighbour(last, "gy", 1)
    right = neighbour(first, "gy", -1)
    result = substep_call(flat, above, below, left, right, flat_velocity, coupling, count, rows, cols)
    return result[0], result[1:]


def exchange_sum(array, axes, last=None):
    stages = []
    for axis in axes:
        count, stride = lax.axis_size(axis), 1
        while stride < count:
            stages.append((axis, stride))
            stride *= 2
    if last in stages:
        stages.remove(last)
        stages.append(last)
    for axis, stride in stages:
        pairs = [(i, i ^ stride) for i in range(lax.axis_size(axis))]
        array = array + lax.ppermute(array, axis, pairs)
    return array


def hdot(a, b):
    return jnp.dot(a, b, precision=lax.Precision.HIGHEST)


def inverse_kernel(a_ref, x_ref, *, size):
    sub = lax.broadcasted_iota(jnp.int32, (size, size), 0)
    lane = lax.broadcasted_iota(jnp.int32, (size, size), 1)
    lane_row = lax.broadcasted_iota(jnp.int32, (1, size), 1)
    sub_col = lax.broadcasted_iota(jnp.int32, (size, 1), 0)

    def row_at(m, k):
        return jnp.sum(jnp.where(sub == k, m, 0.0), axis=0, keepdims=True)

    def col_at(m, k):
        return jnp.sum(jnp.where(lane == k, m, 0.0), axis=1, keepdims=True)

    def lane_at(v, k):
        return jnp.sum(jnp.where(lane_row == k, v, 0.0), axis=1, keepdims=True)

    def step(k, carry):
        a, x, row, col, x_raw = carry
        scale = 1.0 / jnp.sqrt(lane_at(row, k))
        cross = lane_at(row, k + 1) * scale
        low_row = jnp.where(lane_row >= k, row, 0.0) * scale
        low_col = jnp.where(sub_col >= k, col, 0.0) * scale
        x_row = x_raw * scale
        next_row = row_at(a, k + 1) - cross * low_row
        next_col = col_at(a, k + 1) - cross * low_col
        next_x = row_at(x, k + 1) - cross * x_row
        a = a - low_col * low_row
        x = jnp.where(sub == k, x_row, x - jnp.where(sub_col > k, low_col, 0.0) * x_row)
        return a, x, next_row, next_col, next_x

    a0 = a_ref[...]
    eye = jnp.where(sub == lane, 1.0, 0.0).astype(jnp.float32)
    init = (a0, eye, row_at(a0, 0), col_at(a0, 0), row_at(eye, 0))
    x = lax.fori_loop(0, size, step, init, unroll=4)[1]
    x_ref[...] = x


def lower_inverse_call(matrix):
    size = matrix.shape[0]
    vmem = pl.BlockSpec(memory_space=pltpu.VMEM)
    return pl.pallas_call(
        functools.partial(inverse_kernel, size=size),
        out_shape=jax.ShapeDtypeStruct((size, size), jnp.float32),
        in_specs=[vmem],
        out_specs=vmem,
    )(matrix)

def lower_inverse(matrix):
    return lower_inverse_call(0.5 * (matrix + matrix.T))


def body(basis_fields, carried_fields, velocity, diffusion, advection):
    basis_rank, tile_rows, tile_cols = carried_fields.shape
    tile_cells = tile_rows * tile_cols
    aug_count = 2 * basis_rank
    cell_weight = 1.0 / (tile_cells * lax.axis_size("gx") * lax.axis_size("gy"))
    axes = ("gy", "gx")
    flat_basis = basis_fields.reshape(basis_rank, tile_cells)
    flat_carried = carried_fields.reshape(basis_rank, tile_cells)
    known = jnp.concatenate([flat_basis, flat_carried], 0)
    basis_sum = exchange_sum(hdot(flat_basis, known.T), axes) * cell_weight
    flat_velocity = velocity.reshape(2 * tile_rows, tile_cols)
    coupling = jnp.concatenate([diffusion.T, -advection.T], 1)
    shape = (basis_rank, tile_rows, tile_cols)
    carried_rows = carried_fields.reshape(basis_rank * tile_rows, tile_cols)
    edges = edges_call(carried_rows, *shape)
    section_one, edges = one_substep(carried_rows, edges, flat_velocity, coupling, *shape)
    section_two, _ = one_substep(section_one, edges, flat_velocity, coupling, *shape)
    flat_new = section_two.reshape(basis_rank, tile_cells)
    every = jnp.concatenate([flat_basis, flat_new, flat_carried], 0)
    new_sum = exchange_sum(hdot(flat_new, every.T), axes, last=("gy", 1)) * cell_weight
    inverse_11 = lower_inverse(basis_sum[:, :basis_rank])
    low_21 = hdot(new_sum[:, :basis_rank], inverse_11.T)
    schur = new_sum[:, basis_rank:aug_count] - hdot(low_21, low_21.T)
    inverse_22 = lower_inverse(schur)
    top = hdot(inverse_11, flat_basis)
    bottom = hdot(inverse_22, flat_new - hdot(low_21, top))
    new_basis = jnp.concatenate([top, bottom], 0)
    galerkin_top = hdot(inverse_11, basis_sum[:, basis_rank:])
    galerkin_bottom = hdot(inverse_22, new_sum[:, aug_count:] - hdot(low_21, galerkin_top))
    galerkin = jnp.concatenate([galerkin_top, galerkin_bottom], 0)
    return (new_basis.reshape(aug_count, tile_rows, tile_cols), galerkin)


def solution(mesh):
    in_specs = (P(None, "gx", "gy"), P(None, "gx", "gy"), P(None, "gx", "gy"), P(), P())
    out_specs = (P(None, "gx", "gy"), P())
    return jax.shard_map(body, mesh=mesh, in_specs=in_specs, out_specs=out_specs, check_vma=False)
```

```python
import functools
import jax
import jax.numpy as jnp
from jax import lax
from jax.experimental import pallas as pl
from jax.experimental.pallas import tpu as pltpu
from jax.sharding import PartitionSpec as P


def neighbour(array, axis, step):
    count = lax.axis_size(axis)
    pairs = [(i, (i + step) % count) for i in range(count)]
    return lax.ppermute(array, axis, pairs)


def keep_edges(r, block, top_ref, bottom_ref, first_ref, last_ref, rows, cols):
    if r == 0:
        top_ref[...] = block
    if r == rows - 1:
        bottom_ref[...] = block
    first_ref[:, r:r + 1] = block[:, 0:1]
    last_ref[:, r:r + 1] = block[:, cols - 1:cols]


def edges_kernel(f_ref, top_ref, bottom_ref, first_ref, last_ref, *, count, rows, cols):
    row_lane = lax.broadcasted_iota(jnp.int32, (count, rows), 1)
    firsts = jnp.zeros((count, rows), jnp.float32)
    lasts = jnp.zeros((count, rows), jnp.float32)
    for r in range(rows):
        block = f_ref[pl.ds(r, count, stride=rows), :]
        if r == 0:
            top_ref[...] = block
        if r == rows - 1:
            bottom_ref[...] = block
        firsts = jnp.where(row_lane == r, block[:, 0:1], firsts)
        lasts = jnp.where(row_lane == r, block[:, cols - 1:cols], lasts)
    first_ref[...] = firsts
    last_ref[...] = lasts


def substep_kernel(f_ref, above_ref, below_ref, left_ref, right_ref, vel_ref, mix_ref, out_ref,
                   top_ref, bottom_ref, first_ref, last_ref, *, count, rows, cols):
    col_id = lax.broadcasted_iota(jnp.int32, (count, cols), 1)
    coupling = mix_ref[...]

    def row_of(r):
        if r < 0:
            return above_ref[...]
        if r >= rows:
            return below_ref[...]
        return f_ref[pl.ds(r, count, stride=rows), :]

    row_lane = lax.broadcasted_iota(jnp.int32, (count, rows), 1)
    firsts = jnp.zeros((count, rows), jnp.float32)
    lasts = jnp.zeros((count, rows), jnp.float32)
    prev, here = row_of(-1), row_of(0)
    for r in range(rows):
        nxt = row_of(r + 1)
        west = left_ref[:, r:r + 1]
        east = right_ref[:, r:r + 1]
        minus_y = jnp.where(col_id == 0, west, pltpu.roll(here, 1, 1))
        plus_y = jnp.where(col_id == cols - 1, east, pltpu.roll(here, cols - 1, 1))
        speed_x = vel_ref[r:r + 1, :]
        speed_y = vel_ref[rows + r:rows + r + 1, :]
        laplace = nxt + prev + plus_y + minus_y - 4.0 * here
        transport = speed_x * (nxt - prev) * 0.5 + speed_y * (plus_y - minus_y) * 0.5
        rate = jnp.dot(coupling, jnp.concatenate([laplace, transport], 0),
                       precision=lax.Precision.HIGHEST, preferred_element_type=jnp.float32)
        result = here + rate
        out_ref[pl.ds(r, count, stride=rows), :] = result
        if r == 0:
            top_ref[...] = result
        if r == rows - 1:
            bottom_ref[...] = result
        firsts = jnp.where(row_lane == r, result[:, 0:1], firsts)
        lasts = jnp.where(row_lane == r, result[:, cols - 1:cols], lasts)
        prev, here = here, nxt
    first_ref[...] = firsts
    last_ref[...] = lasts


def edge_shapes(count, rows, cols):
    return [
        jax.ShapeDtypeStruct((count, cols), jnp.float32),
        jax.ShapeDtypeStruct((count, cols), jnp.float32),
        jax.ShapeDtypeStruct((count, rows), jnp.float32),
        jax.ShapeDtypeStruct((count, rows), jnp.float32),
    ]


def edges_call(flat, count, rows, cols):
    vmem = pl.BlockSpec(memory_space=pltpu.VMEM)
    return pl.pallas_call(
        functools.partial(edges_kernel, count=count, rows=rows, cols=cols),
        out_shape=edge_shapes(count, rows, cols),
        in_specs=[vmem],
        out_specs=[vmem] * 4,
    )(flat)


def substep_call(flat, above, below, left, right, vel, coupling, count, rows, cols):
    vmem = pl.BlockSpec(memory_space=pltpu.VMEM)
    return pl.pallas_call(
        functools.partial(substep_kernel, count=count, rows=rows, cols=cols),
        out_shape=[jax.ShapeDtypeStruct((count * rows, cols), jnp.float32)]
        + edge_shapes(count, rows, cols),
        in_specs=[vmem] * 7,
        out_specs=[vmem] * 5,
    )(flat, above, below, left, right, vel, coupling)


def one_substep(flat, edges, flat_velocity, coupling, count, rows, cols):
    top, bottom, first, last = edges
    above = neighbour(bottom, "gx", 1)
    below = neighbour(top, "gx", -1)
    left = neighbour(last, "gy", 1)
    right = neighbour(first, "gy", -1)
    result = substep_call(flat, above, below, left, right, flat_velocity, coupling, count, rows, cols)
    return result[0], result[1:]


def exchange_sum(array, axes, last=None):
    stages = []
    for axis in axes:
        count, stride = lax.axis_size(axis), 1
        while stride < count:
            stages.append((axis, stride))
            stride *= 2
    if last in stages:
        stages.remove(last)
        stages.append(last)
    for axis, stride in stages:
        pairs = [(i, i ^ stride) for i in range(lax.axis_size(axis))]
        array = array + lax.ppermute(array, axis, pairs)
    return array


def hdot(a, b):
    return jnp.dot(a, b, precision=lax.Precision.HIGHEST)


def inverse_kernel(a_ref, x_ref, *, size):
    sub = lax.broadcasted_iota(jnp.int32, (size, size), 0)
    lane = lax.broadcasted_iota(jnp.int32, (size, size), 1)
    lane_row = lax.broadcasted_iota(jnp.int32, (1, size), 1)
    sub_col = lax.broadcasted_iota(jnp.int32, (size, 1), 0)

    def row_at(m, k):
        return jnp.sum(jnp.where(sub == k, m, 0.0), axis=0, keepdims=True)

    def col_at(m, k):
        return jnp.sum(jnp.where(lane == k, m, 0.0), axis=1, keepdims=True)

    def lane_at(v, k):
        return jnp.sum(jnp.where(lane_row == k, v, 0.0), axis=1, keepdims=True)

    def step(k, carry):
        a, x, row, col, x_raw = carry
        scale = 1.0 / jnp.sqrt(lane_at(row, k))
        cross = lane_at(row, k + 1) * scale
        low_row = jnp.where(lane_row >= k, row, 0.0) * scale
        low_col = jnp.where(sub_col >= k, col, 0.0) * scale
        x_row = x_raw * scale
        next_row = row_at(a, k + 1) - cross * low_row
        next_col = col_at(a, k + 1) - cross * low_col
        next_x = row_at(x, k + 1) - cross * x_row
        a = a - low_col * low_row
        x = jnp.where(sub == k, x_row, x - jnp.where(sub_col > k, low_col, 0.0) * x_row)
        return a, x, next_row, next_col, next_x

    a0 = a_ref[...]
    eye = jnp.where(sub == lane, 1.0, 0.0).astype(jnp.float32)
    init = (a0, eye, row_at(a0, 0), col_at(a0, 0), row_at(eye, 0))
    x = lax.fori_loop(0, size, step, init, unroll=4)[1]
    x_ref[...] = x


def lower_inverse_call(matrix):
    size = matrix.shape[0]
    vmem = pl.BlockSpec(memory_space=pltpu.VMEM)
    return pl.pallas_call(
        functools.partial(inverse_kernel, size=size),
        out_shape=jax.ShapeDtypeStruct((size, size), jnp.float32),
        in_specs=[vmem],
        out_specs=vmem,
    )(matrix)

def lower_inverse(matrix):
    return lower_inverse_call(0.5 * (matrix + matrix.T))


def body(basis_fields, carried_fields, velocity, diffusion, advection):
    basis_rank, tile_rows, tile_cols = carried_fields.shape
    tile_cells = tile_rows * tile_cols
    aug_count = 2 * basis_rank
    cell_weight = 1.0 / (tile_cells * lax.axis_size("gx") * lax.axis_size("gy"))
    axes = ("gy", "gx")
    flat_basis = basis_fields.reshape(basis_rank, tile_cells)
    flat_carried = carried_fields.reshape(basis_rank, tile_cells)
    known = jnp.concatenate([flat_basis, flat_carried], 0)
    basis_sum = exchange_sum(hdot(flat_basis, known.T), axes) * cell_weight
    flat_velocity = velocity.reshape(2 * tile_rows, tile_cols)
    coupling = jnp.concatenate([diffusion.T, -advection.T], 1)
    shape = (basis_rank, tile_rows, tile_cols)
    carried_rows = carried_fields.reshape(basis_rank * tile_rows, tile_cols)
    edges = edges_call(carried_rows, *shape)
    section_one, edges = one_substep(carried_rows, edges, flat_velocity, coupling, *shape)
    section_two, _ = one_substep(section_one, edges, flat_velocity, coupling, *shape)
    flat_new = section_two.reshape(basis_rank, tile_cells)
    every = jnp.concatenate([flat_basis, flat_new, flat_carried], 0)
    new_sum = exchange_sum(hdot(flat_new, every.T), axes, last=("gy", 1)) * cell_weight
    inverse_11 = lower_inverse(basis_sum[:, :basis_rank])
    low_21 = hdot(new_sum[:, :basis_rank], inverse_11.T)
    schur = new_sum[:, basis_rank:aug_count] - hdot(low_21, low_21.T)
    inverse_22 = lower_inverse(schur)
    top = hdot(inverse_11, flat_basis)
    bottom = hdot(inverse_22, flat_new - hdot(low_21, top))
    new_basis = jnp.concatenate([top, bottom], 0)
    galerkin_top = hdot(inverse_11, basis_sum[:, basis_rank:])
    galerkin_bottom = hdot(inverse_22, new_sum[:, aug_count:] - hdot(low_21, galerkin_top))
    galerkin = jnp.concatenate([galerkin_top, galerkin_bottom], 0)
    return (new_basis.reshape(aug_count, tile_rows, tile_cols), galerkin)


def solution(mesh):
    in_specs = (P(None, "gx", "gy"), P(None, "gx", "gy"), P(None, "gx", "gy"), P(), P())
    out_specs = (P(None, "gx", "gy"), P())
    return jax.shard_map(body, mesh=mesh, in_specs=in_specs, out_specs=out_specs, check_vma=False)
```

```python
import functools
import jax
import jax.numpy as jnp
from jax import lax
from jax.experimental import pallas as pl
from jax.experimental.pallas import tpu as pltpu
from jax.sharding import PartitionSpec as P


def neighbour(array, axis, step):
    count = lax.axis_size(axis)
    pairs = [(i, (i + step) % count) for i in range(count)]
    return lax.ppermute(array, axis, pairs)


def keep_edges(r, block, top_ref, bottom_ref, first_ref, last_ref, rows, cols):
    if r == 0:
        top_ref[...] = block
    if r == rows - 1:
        bottom_ref[...] = block
    first_ref[:, r:r + 1] = block[:, 0:1]
    last_ref[:, r:r + 1] = block[:, cols - 1:cols]


def edges_kernel(f_ref, top_ref, bottom_ref, first_ref, last_ref, *, count, rows, cols):
    row_lane = lax.broadcasted_iota(jnp.int32, (count, rows), 1)
    firsts = jnp.zeros((count, rows), jnp.float32)
    lasts = jnp.zeros((count, rows), jnp.float32)
    for r in range(rows):
        block = f_ref[pl.ds(r, count, stride=rows), :]
        if r == 0:
            top_ref[...] = block
        if r == rows - 1:
            bottom_ref[...] = block
        firsts = jnp.where(row_lane == r, block[:, 0:1], firsts)
        lasts = jnp.where(row_lane == r, block[:, cols - 1:cols], lasts)
    first_ref[...] = firsts
    last_ref[...] = lasts


def substep_kernel(f_ref, above_ref, below_ref, left_ref, right_ref, vel_ref, mix_ref, out_ref,
                   top_ref, bottom_ref, first_ref, last_ref, *, count, rows, cols):
    col_id = lax.broadcasted_iota(jnp.int32, (count, cols), 1)
    coupling = mix_ref[...]

    def row_of(r):
        if r < 0:
            return above_ref[...]
        if r >= rows:
            return below_ref[...]
        return f_ref[pl.ds(r, count, stride=rows), :]

    prev, here = row_of(-1), row_of(0)
    for r in range(rows):
        nxt = row_of(r + 1)
        west = left_ref[:, r:r + 1]
        east = right_ref[:, r:r + 1]
        minus_y = jnp.where(col_id == 0, west, pltpu.roll(here, 1, 1))
        plus_y = jnp.where(col_id == cols - 1, east, pltpu.roll(here, cols - 1, 1))
        speed_x = vel_ref[r:r + 1, :]
        speed_y = vel_ref[rows + r:rows + r + 1, :]
        laplace = nxt + prev + plus_y + minus_y - 4.0 * here
        transport = speed_x * (nxt - prev) * 0.5 + speed_y * (plus_y - minus_y) * 0.5
        rate = jnp.dot(coupling, jnp.concatenate([laplace, transport], 0),
                       precision=lax.Precision.HIGHEST, preferred_element_type=jnp.float32)
        result = here + rate
        out_ref[pl.ds(r, count, stride=rows), :] = result
        keep_edges(r, result, top_ref, bottom_ref, first_ref, last_ref, rows, cols)
        prev, here = here, nxt


def edge_shapes(count, rows, cols):
    return [
        jax.ShapeDtypeStruct((count, cols), jnp.float32),
        jax.ShapeDtypeStruct((count, cols), jnp.float32),
        jax.ShapeDtypeStruct((count, rows), jnp.float32),
        jax.ShapeDtypeStruct((count, rows), jnp.float32),
    ]


def edges_call(flat, count, rows, cols):
    vmem = pl.BlockSpec(memory_space=pltpu.VMEM)
    return pl.pallas_call(
        functools.partial(edges_kernel, count=count, rows=rows, cols=cols),
        out_shape=edge_shapes(count, rows, cols),
        in_specs=[vmem],
        out_specs=[vmem] * 4,
    )(flat)


def substep_call(flat, above, below, left, right, vel, coupling, count, rows, cols):
    vmem = pl.BlockSpec(memory_space=pltpu.VMEM)
    return pl.pallas_call(
        functools.partial(substep_kernel, count=count, rows=rows, cols=cols),
        out_shape=[jax.ShapeDtypeStruct((count * rows, cols), jnp.float32)]
        + edge_shapes(count, rows, cols),
        in_specs=[vmem] * 7,
        out_specs=[vmem] * 5,
    )(flat, above, below, left, right, vel, coupling)


def one_substep(flat, edges, flat_velocity, coupling, count, rows, cols):
    top, bottom, first, last = edges
    above = neighbour(bottom, "gx", 1)
    below = neighbour(top, "gx", -1)
    left = neighbour(last, "gy", 1)
    right = neighbour(first, "gy", -1)
    result = substep_call(flat, above, below, left, right, flat_velocity, coupling, count, rows, cols)
    return result[0], result[1:]


def exchange_sum(array, axes, last=None, first=None):
    stages = []
    for axis in axes:
        count, stride = lax.axis_size(axis), 1
        while stride < count:
            stages.append((axis, stride))
            stride *= 2
    if last in stages:
        stages.remove(last)
        stages.append(last)
    if first in stages:
        stages.remove(first)
        stages.insert(0, first)
    for axis, stride in stages:
        pairs = [(i, i ^ stride) for i in range(lax.axis_size(axis))]
        array = array + lax.ppermute(array, axis, pairs)
    return array


def hdot(a, b):
    return jnp.dot(a, b, precision=lax.Precision.HIGHEST)


def inverse_kernel(a_ref, x_ref, *, size):
    sub = lax.broadcasted_iota(jnp.int32, (size, size), 0)
    lane = lax.broadcasted_iota(jnp.int32, (size, size), 1)
    lane_row = lax.broadcasted_iota(jnp.int32, (1, size), 1)
    sub_col = lax.broadcasted_iota(jnp.int32, (size, 1), 0)

    def row_at(m, k):
        return jnp.sum(jnp.where(sub == k, m, 0.0), axis=0, keepdims=True)

    def col_at(m, k):
        return jnp.sum(jnp.where(lane == k, m, 0.0), axis=1, keepdims=True)

    def lane_at(v, k):
        return jnp.sum(jnp.where(lane_row == k, v, 0.0), axis=1, keepdims=True)

    def step(k, carry):
        a, x, row, col, x_raw = carry
        scale = 1.0 / jnp.sqrt(lane_at(row, k))
        cross = lane_at(row, k + 1) * scale
        low_row = jnp.where(lane_row >= k, row, 0.0) * scale
        low_col = jnp.where(sub_col >= k, col, 0.0) * scale
        x_row = x_raw * scale
        next_row = row_at(a, k + 1) - cross * low_row
        next_col = col_at(a, k + 1) - cross * low_col
        next_x = row_at(x, k + 1) - cross * x_row
        a = a - low_col * low_row
        x = jnp.where(sub == k, x_row, x - jnp.where(sub_col > k, low_col, 0.0) * x_row)
        return a, x, next_row, next_col, next_x

    a0 = a_ref[...]
    eye = jnp.where(sub == lane, 1.0, 0.0).astype(jnp.float32)
    init = (a0, eye, row_at(a0, 0), col_at(a0, 0), row_at(eye, 0))
    x = lax.fori_loop(0, size, step, init, unroll=4)[1]
    x_ref[...] = x


def lower_inverse_call(matrix):
    size = matrix.shape[0]
    vmem = pl.BlockSpec(memory_space=pltpu.VMEM)
    return pl.pallas_call(
        functools.partial(inverse_kernel, size=size),
        out_shape=jax.ShapeDtypeStruct((size, size), jnp.float32),
        in_specs=[vmem],
        out_specs=vmem,
    )(matrix)

def lower_inverse(matrix):
    return lower_inverse_call(0.5 * (matrix + matrix.T))


def body(basis_fields, carried_fields, velocity, diffusion, advection):
    basis_rank, tile_rows, tile_cols = carried_fields.shape
    tile_cells = tile_rows * tile_cols
    aug_count = 2 * basis_rank
    cell_weight = 1.0 / (tile_cells * lax.axis_size("gx") * lax.axis_size("gy"))
    axes = ("gy", "gx")
    flat_basis = basis_fields.reshape(basis_rank, tile_cells)
    flat_carried = carried_fields.reshape(basis_rank, tile_cells)
    known = jnp.concatenate([flat_basis, flat_carried], 0)
    basis_sum = exchange_sum(hdot(flat_basis, known.T), axes) * cell_weight
    flat_velocity = velocity.reshape(2 * tile_rows, tile_cols)
    coupling = jnp.concatenate([diffusion.T, -advection.T], 1)
    shape = (basis_rank, tile_rows, tile_cols)
    carried_rows = carried_fields.reshape(basis_rank * tile_rows, tile_cols)
    edges = edges_call(carried_rows, *shape)
    section_one, edges = one_substep(carried_rows, edges, flat_velocity, coupling, *shape)
    section_two, _ = one_substep(section_one, edges, flat_velocity, coupling, *shape)
    flat_new = section_two.reshape(basis_rank, tile_cells)
    every = jnp.concatenate([flat_basis, flat_new, flat_carried], 0)
    new_sum = exchange_sum(hdot(flat_new, every.T), axes, last=("gy", 1), first=("gy", 4)) * cell_weight
    inverse_11 = lower_inverse(basis_sum[:, :basis_rank])
    low_21 = hdot(new_sum[:, :basis_rank], inverse_11.T)
    schur = new_sum[:, basis_rank:aug_count] - hdot(low_21, low_21.T)
    inverse_22 = lower_inverse(schur)
    top = hdot(inverse_11, flat_basis)
    bottom = hdot(inverse_22, flat_new - hdot(low_21, top))
    new_basis = jnp.concatenate([top, bottom], 0)
    galerkin_top = hdot(inverse_11, basis_sum[:, basis_rank:])
    galerkin_bottom = hdot(inverse_22, new_sum[:, aug_count:] - hdot(low_21, galerkin_top))
    galerkin = jnp.concatenate([galerkin_top, galerkin_bottom], 0)
    return (new_basis.reshape(aug_count, tile_rows, tile_cols), galerkin)


def solution(mesh):
    in_specs = (P(None, "gx", "gy"), P(None, "gx", "gy"), P(None, "gx", "gy"), P(), P())
    out_specs = (P(None, "gx", "gy"), P())
    return jax.shard_map(body, mesh=mesh, in_specs=in_specs, out_specs=out_specs, check_vma=False)
```

```python
import functools
import jax
import jax.numpy as jnp
from jax import lax
from jax.experimental import pallas as pl
from jax.experimental.pallas import tpu as pltpu
from jax.sharding import PartitionSpec as P


def neighbour(array, axis, step):
    count = lax.axis_size(axis)
    pairs = [(i, (i + step) % count) for i in range(count)]
    return lax.ppermute(array, axis, pairs)


def keep_edges(r, block, top_ref, bottom_ref, first_ref, last_ref, rows, cols):
    if r == 0:
        top_ref[...] = block
    if r == rows - 1:
        bottom_ref[...] = block
    first_ref[:, r:r + 1] = block[:, 0:1]
    last_ref[:, r:r + 1] = block[:, cols - 1:cols]


def edges_kernel(f_ref, top_ref, bottom_ref, first_ref, last_ref, *, count, rows, cols):
    row_lane = lax.broadcasted_iota(jnp.int32, (count, rows), 1)
    firsts = jnp.zeros((count, rows), jnp.float32)
    lasts = jnp.zeros((count, rows), jnp.float32)
    for r in range(rows):
        block = f_ref[pl.ds(r, count, stride=rows), :]
        if r == 0:
            top_ref[...] = block
        if r == rows - 1:
            bottom_ref[...] = block
        firsts = jnp.where(row_lane == r, block[:, 0:1], firsts)
        lasts = jnp.where(row_lane == r, block[:, cols - 1:cols], lasts)
    first_ref[...] = firsts
    last_ref[...] = lasts


def substep_kernel(f_ref, above_ref, below_ref, left_ref, right_ref, vel_ref, mix_ref, out_ref,
                   top_ref, bottom_ref, first_ref, last_ref, *, count, rows, cols):
    col_id = lax.broadcasted_iota(jnp.int32, (count, cols), 1)
    coupling = mix_ref[...]

    def row_of(r):
        if r < 0:
            return above_ref[...]
        if r >= rows:
            return below_ref[...]
        return f_ref[pl.ds(r, count, stride=rows), :]

    prev, here = row_of(-1), row_of(0)
    for r in range(rows):
        nxt = row_of(r + 1)
        west = left_ref[:, r:r + 1]
        east = right_ref[:, r:r + 1]
        minus_y = jnp.where(col_id == 0, west, pltpu.roll(here, 1, 1))
        plus_y = jnp.where(col_id == cols - 1, east, pltpu.roll(here, cols - 1, 1))
        speed_x = vel_ref[r:r + 1, :]
        speed_y = vel_ref[rows + r:rows + r + 1, :]
        laplace = nxt + prev + plus_y + minus_y - 4.0 * here
        transport = speed_x * (nxt - prev) * 0.5 + speed_y * (plus_y - minus_y) * 0.5
        rate = jnp.dot(coupling, jnp.concatenate([laplace, transport], 0),
                       precision=lax.Precision.HIGHEST, preferred_element_type=jnp.float32)
        result = here + rate
        out_ref[pl.ds(r, count, stride=rows), :] = result
        keep_edges(r, result, top_ref, bottom_ref, first_ref, last_ref, rows, cols)
        prev, here = here, nxt


def edge_shapes(count, rows, cols):
    return [
        jax.ShapeDtypeStruct((count, cols), jnp.float32),
        jax.ShapeDtypeStruct((count, cols), jnp.float32),
        jax.ShapeDtypeStruct((count, rows), jnp.float32),
        jax.ShapeDtypeStruct((count, rows), jnp.float32),
    ]


def edges_call(flat, count, rows, cols):
    vmem = pl.BlockSpec(memory_space=pltpu.VMEM)
    return pl.pallas_call(
        functools.partial(edges_kernel, count=count, rows=rows, cols=cols),
        out_shape=edge_shapes(count, rows, cols),
        in_specs=[vmem],
        out_specs=[vmem] * 4,
    )(flat)


def substep_call(flat, above, below, left, right, vel, coupling, count, rows, cols):
    vmem = pl.BlockSpec(memory_space=pltpu.VMEM)
    return pl.pallas_call(
        functools.partial(substep_kernel, count=count, rows=rows, cols=cols),
        out_shape=[jax.ShapeDtypeStruct((count * rows, cols), jnp.float32)]
        + edge_shapes(count, rows, cols),
        in_specs=[vmem] * 7,
        out_specs=[vmem] * 5,
    )(flat, above, below, left, right, vel, coupling)


def one_substep(flat, edges, flat_velocity, coupling, count, rows, cols):
    top, bottom, first, last = edges
    above = neighbour(bottom, "gx", 1)
    below = neighbour(top, "gx", -1)
    left = neighbour(last, "gy", 1)
    right = neighbour(first, "gy", -1)
    result = substep_call(flat, above, below, left, right, flat_velocity, coupling, count, rows, cols)
    return result[0], result[1:]


def exchange_sum(array, axes, last=None, hold=None):
    stages = []
    for axis in axes:
        count, stride = lax.axis_size(axis), 1
        while stride < count:
            stages.append((axis, stride))
            stride *= 2
    if last in stages:
        stages.remove(last)
        stages.append(last)
    for number, (axis, stride) in enumerate(stages):
        if number == len(stages) - 1 and hold is not None:
            array, hold = lax.optimization_barrier((array, hold))
        pairs = [(i, i ^ stride) for i in range(lax.axis_size(axis))]
        array = array + lax.ppermute(array, axis, pairs)
    return array if hold is None else (array, hold)


def hdot(a, b):
    return jnp.dot(a, b, precision=lax.Precision.HIGHEST)


def inverse_kernel(a_ref, x_ref, *, size):
    sub = lax.broadcasted_iota(jnp.int32, (size, size), 0)
    lane = lax.broadcasted_iota(jnp.int32, (size, size), 1)
    lane_row = lax.broadcasted_iota(jnp.int32, (1, size), 1)
    sub_col = lax.broadcasted_iota(jnp.int32, (size, 1), 0)

    def row_at(m, k):
        return jnp.sum(jnp.where(sub == k, m, 0.0), axis=0, keepdims=True)

    def col_at(m, k):
        return jnp.sum(jnp.where(lane == k, m, 0.0), axis=1, keepdims=True)

    def lane_at(v, k):
        return jnp.sum(jnp.where(lane_row == k, v, 0.0), axis=1, keepdims=True)

    def step(k, carry):
        a, x, row, col, x_raw = carry
        scale = 1.0 / jnp.sqrt(lane_at(row, k))
        cross = lane_at(row, k + 1) * scale
        low_row = jnp.where(lane_row >= k, row, 0.0) * scale
        low_col = jnp.where(sub_col >= k, col, 0.0) * scale
        x_row = x_raw * scale
        next_row = row_at(a, k + 1) - cross * low_row
        next_col = col_at(a, k + 1) - cross * low_col
        next_x = row_at(x, k + 1) - cross * x_row
        a = a - low_col * low_row
        x = jnp.where(sub == k, x_row, x - jnp.where(sub_col > k, low_col, 0.0) * x_row)
        return a, x, next_row, next_col, next_x

    a0 = a_ref[...]
    eye = jnp.where(sub == lane, 1.0, 0.0).astype(jnp.float32)
    init = (a0, eye, row_at(a0, 0), col_at(a0, 0), row_at(eye, 0))
    x = lax.fori_loop(0, size, step, init, unroll=4)[1]
    x_ref[...] = x


def lower_inverse_call(matrix):
    size = matrix.shape[0]
    vmem = pl.BlockSpec(memory_space=pltpu.VMEM)
    return pl.pallas_call(
        functools.partial(inverse_kernel, size=size),
        out_shape=jax.ShapeDtypeStruct((size, size), jnp.float32),
        in_specs=[vmem],
        out_specs=vmem,
    )(matrix)

def lower_inverse(matrix):
    return lower_inverse_call(0.5 * (matrix + matrix.T))


def body(basis_fields, carried_fields, velocity, diffusion, advection):
    basis_rank, tile_rows, tile_cols = carried_fields.shape
    tile_cells = tile_rows * tile_cols
    aug_count = 2 * basis_rank
    cell_weight = 1.0 / (tile_cells * lax.axis_size("gx") * lax.axis_size("gy"))
    axes = ("gy", "gx")
    flat_basis = basis_fields.reshape(basis_rank, tile_cells)
    flat_carried = carried_fields.reshape(basis_rank, tile_cells)
    known = jnp.concatenate([flat_basis, flat_carried], 0)
    basis_sum = exchange_sum(hdot(flat_basis, known.T), axes) * cell_weight
    flat_velocity = velocity.reshape(2 * tile_rows, tile_cols)
    coupling = jnp.concatenate([diffusion.T, -advection.T], 1)
    shape = (basis_rank, tile_rows, tile_cols)
    carried_rows = carried_fields.reshape(basis_rank * tile_rows, tile_cols)
    edges = edges_call(carried_rows, *shape)
    section_one, edges = one_substep(carried_rows, edges, flat_velocity, coupling, *shape)
    section_two, _ = one_substep(section_one, edges, flat_velocity, coupling, *shape)
    flat_new = section_two.reshape(basis_rank, tile_cells)
    every = jnp.concatenate([flat_basis, flat_new, flat_carried], 0)
    inverse_11 = lower_inverse(basis_sum[:, :basis_rank])
    new_sum, inverse_11 = exchange_sum(
        hdot(flat_new, every.T), axes, last=("gy", 1), hold=inverse_11
    )
    new_sum = new_sum * cell_weight
    low_21 = hdot(new_sum[:, :basis_rank], inverse_11.T)
    schur = new_sum[:, basis_rank:aug_count] - hdot(low_21, low_21.T)
    inverse_22 = lower_inverse(schur)
    top = hdot(inverse_11, flat_basis)
    bottom = hdot(inverse_22, flat_new - hdot(low_21, top))
    new_basis = jnp.concatenate([top, bottom], 0)
    galerkin_top = hdot(inverse_11, basis_sum[:, basis_rank:])
    galerkin_bottom = hdot(inverse_22, new_sum[:, aug_count:] - hdot(low_21, galerkin_top))
    galerkin = jnp.concatenate([galerkin_top, galerkin_bottom], 0)
    return (new_basis.reshape(aug_count, tile_rows, tile_cols), galerkin)


def solution(mesh):
    in_specs = (P(None, "gx", "gy"), P(None, "gx", "gy"), P(None, "gx", "gy"), P(), P())
    out_specs = (P(None, "gx", "gy"), P())
    return jax.shard_map(body, mesh=mesh, in_specs=in_specs, out_specs=out_specs, check_vma=False)
```
